256 devices in a mesh: dp: 8 (over z_lo, core), seq: 32 (over z_hi, x, y).
Axes of the slice: x: 4, y: 4, z: 8 (z_hi: 2, z_lo: 4; z = z_hi * 4 + z_lo), core: 2. Of those that a mesh axis runs over, the one named last changes fastest.
Arguments:
- mapped_askers: bfloat16 [8, 8192, 1024], P('dp', 'seq'), may hold values from -6 to 6
- mapped_lookups: bfloat16 [8, 8192, 1024], P('dp', 'seq'), may hold values from -6 to 6
- mapped_contents: bfloat16 [8, 8192, 1024], P('dp', 'seq'), may hold values from -24 to 24
- result_cotangent: bfloat16 [8, 8192, 1024], P('dp', 'seq'), may hold values from -6 to 6
- result_weight_matrix: bfloat16 [1024, 1024], replicated, may hold values from -0.1875 to 0.1875
- reference_comb_shift: int32 [32, 32], P('seq'), may hold values from 0 to 7
- symbol_frame_label: int32 [8192], replicated, may hold values from 0 to 15, never falling along the last dimension, each value on 1 to 1024 neighbouring positions
Outputs:
- sublayer_out: bfloat16 [8, 8192, 1024], P('dp', 'seq')
- query_grad: bfloat16 [8, 8192, 1024], P('dp', 'seq')
- key_grad: bfloat16 [8, 8192, 1024], P('dp', 'seq')
- value_grad: bfloat16 [8, 8192, 1024], P('dp', 'seq')
- weight_grad: float32 [1024, 1024], P(('dp', 'seq'))
The draws below stay inside these ranges and needn't reach their ends.
All inputs are finite; a program needn't handle non-finite values.
Results may differ from the reference program's by a relative error of at most 0.012.
Values may be sent and summed in bfloat16 or wider, within the bound.
No kernel may reach another device: no remote copies, remote signals or barrier semaphores. Data moves between devices by JAX's collectives and lax.ppermute only.
A program may use at most 128 MiB of HBM per device.

```python
import math
import jax
import jax.numpy as jnp
import numpy as np
from jax import lax

D = 1024
HEADS = 8
HALF_SPAN = 256
FRAME_SHARDS = 8
PIECE_SYMBOLS = 256
PIL_SHARD = 32
FRAME_PILOTS = 256
ROUND_SYMBOLS = 8192
FRAMES = 4
PASSES = 8
FRAME_NUMBER = 16
N_SEQ = 32


def paired(key):
    full_shape = (PASSES, ROUND_SYMBOLS, D)
    query_key = jax.random.fold_in(key, 101)
    keys_key = jax.random.fold_in(key, 102)
    mapped_askers = jnp.clip(1.1 * jax.random.normal(query_key, full_shape, jnp.float32), -6.0, 6.0)
    keyset = jnp.clip(1.1 * jax.random.normal(keys_key, full_shape, jnp.float32), -6.0, 6.0)
    return (mapped_askers, keyset)


def draw_mapped_askers(key, part):
    return paired(key)[0].astype(jnp.bfloat16)


def draw_mapped_lookups(key, part):
    return paired(key)[1].astype(jnp.bfloat16)


def place_ends(values, own_key, low, top_value):
    place = [jax.random.randint(jax.random.fold_in(own_key, axis), (), 0, length) for axis, length in enumerate(values.shape)]
    main_axis = values.shape.index(max(values.shape))
    beside = place[:main_axis] + [(place[main_axis] + 1) % values.shape[main_axis]] + place[main_axis + 1:]
    return values.at[tuple(place)].set(low).at[tuple(beside)].set(top_value)


def shard_levels(key, dims, shards, smallest, high):
    def one(dim, shards_of):
        draws = jax.random.uniform(jax.random.fold_in(jax.random.fold_in(key, 6), dim), (shards_of,), jnp.float32, smallest / len(shards), high / len(shards))
        return jnp.repeat(jnp.exp(draws), dims[dim] // shards_of).reshape((-1,) + (1,) * (len(dims) - dim - 1))

    factor_of = one(*shards[0])
    for cut in shards[1:]:
        factor_of = factor_of * one(*cut)
    return factor_of


def profile(count, total, most, slope):
    portions = [(1 << 20) // math.isqrt(grade ** slope) + 1 for grade in range(2, count + 1)]
    spare, holding = total - most - (count - 1), [1] * (count - 1)
    while spare > 0:
        free = [i for i in range(count - 1) if holding[i] < most]
        pool, budget = sum([portions[i] for i in free]), spare
        for i in free:
            more = min(most - holding[i], max(1, budget * portions[i] // pool), spare)
            holding[i] = holding[i] + more
            spare = spare - more
    return np.array([most] + holding)


def ragged(rng, number_of, total, reach, slope):
    if number_of == 2:
        one = jax.random.randint(rng, (), max(1, total - reach), min(reach, total - 1) + 1)
        return jnp.stack([one, total - one])
    tallies = jnp.asarray(profile(number_of, total, reach, slope), jnp.int32)
    couples = (number_of - 1) // 2
    source_of, taker = tallies[1:1 + 2 * couples:2], tallies[2:2 + 2 * couples:2]
    room = jnp.minimum(source_of - 1, reach - taker)
    moved = jax.random.randint(jax.random.fold_in(rng, 1), (couples,), 0, 1 << 20) % (room + 1)
    tallies = tallies.at[1:1 + 2 * couples:2].set(source_of - moved).at[2:2 + 2 * couples:2].set(taker + moved)
    return tallies[jax.random.permutation(jax.random.fold_in(rng, 2), number_of)]


def bell_draw(stream_key, dims, width, reach, shards=(), kind=jnp.bfloat16):
    level = shard_levels(stream_key, dims, shards, -0.22, 0.18) if shards else 1.0
    entries = jax.random.normal(stream_key, dims, jnp.float32) * width * level
    return jnp.minimum(jnp.maximum(entries, -reach), reach).astype(kind)


def setup_inputs(seed: int = 0) -> dict:
    streams_of = jax.random.split(jax.random.key(seed), 8)
    mapped_askers = draw_mapped_askers(jax.random.fold_in(streams_of[7], 71), 0)
    mapped_lookups = draw_mapped_lookups(jax.random.fold_in(streams_of[7], 71), 0)
    mapped_contents = bell_draw(streams_of[2], (PASSES, ROUND_SYMBOLS, D), 4.0, 24.0, ((0, 8), (1, 32)))
    result_cotangent = bell_draw(streams_of[3], (PASSES, ROUND_SYMBOLS, D), 1.0, 6.0, ((0, 8), (1, 32)))
    result_weight_matrix = bell_draw(streams_of[4], (D, D), D ** -0.5, 0.1875)
    reference_comb_shift = place_ends(jax.random.randint(streams_of[5], (N_SEQ, PIL_SHARD), 0, PIECE_SYMBOLS // PIL_SHARD), jax.random.fold_in(streams_of[5], 1), 0, (PIECE_SYMBOLS // PIL_SHARD) - 1).astype(jnp.int32)
    symbol_frame_label = jnp.searchsorted(jnp.cumsum(ragged(streams_of[6], FRAME_NUMBER, ROUND_SYMBOLS, 4 * PIECE_SYMBOLS, 1)), jnp.arange(ROUND_SYMBOLS), side="right").astype(jnp.int32)
    return dict(mapped_askers=mapped_askers, mapped_lookups=mapped_lookups, mapped_contents=mapped_contents, result_cotangent=result_cotangent, result_weight_matrix=result_weight_matrix, reference_comb_shift=reference_comb_shift, symbol_frame_label=symbol_frame_label)


def joint_admit_filter(neighbor_frame_label, overall_line_number):
    query_rows = jnp.arange(overall_line_number)[:, None] + HALF_SPAN
    key_cols = jnp.arange(overall_line_number + 2 * HALF_SPAN)[None, :]
    inside_local_distance = jnp.abs(query_rows - key_cols) <= HALF_SPAN
    asker_frame_label = neighbor_frame_label[HALF_SPAN:HALF_SPAN + overall_line_number]
    same_frame_filter = asker_frame_label[:, None] == neighbor_frame_label[None, :]
    return inside_local_distance & same_frame_filter

def attend_shard(query_block, key_win, val_win, key_pil, val_pil, local_admit_filter, grad_att):
    head_dim = query_block.shape[1] // HEADS
    scaling = 1.0 / math.sqrt(head_dim)

    def split_heads(matrix):
        return jnp.transpose(matrix.reshape(matrix.shape[0], HEADS, head_dim), (1, 0, 2))

    def join_heads(matrix):
        return jnp.transpose(matrix, (1, 0, 2)).reshape(matrix.shape[1], HEADS * head_dim)

    def one_head(round_arguments):
        query_head, key_head, val_head, pilot_key, pilot_val, grad_head = round_arguments
        score_win = jnp.dot(query_head, key_head.T, preferred_element_type=jnp.float32) * scaling
        score_win = jnp.where(local_admit_filter, score_win, -jnp.inf)
        score_pil = jnp.dot(query_head, pilot_key.T, preferred_element_type=jnp.float32) * scaling
        row_max = jnp.maximum(lax.optimization_barrier(jnp.max(score_win, axis=1)), lax.optimization_barrier(jnp.max(score_pil, axis=1)))[:, None]
        exp_win = jnp.exp(score_win - row_max)
        exp_pil = jnp.exp(score_pil - row_max)
        softmax_total = lax.optimization_barrier(jnp.sum(exp_win, axis=1, keepdims=True)) + lax.optimization_barrier(jnp.sum(exp_pil, axis=1, keepdims=True))
        prob_win = exp_win / softmax_total
        prob_pil = exp_pil / softmax_total
        weight_win = prob_win.astype(jnp.bfloat16)
        weight_pil = prob_pil.astype(jnp.bfloat16)
        attended = (jnp.dot(weight_win, val_head, preferred_element_type=jnp.float32) + jnp.dot(weight_pil, pilot_val, preferred_element_type=jnp.float32)).astype(jnp.bfloat16)
        dprob_win = jnp.dot(grad_head, val_head.T, preferred_element_type=jnp.float32)
        dprob_pil = jnp.dot(grad_head, pilot_val.T, preferred_element_type=jnp.float32)
        delta = lax.optimization_barrier(jnp.sum(grad_head.astype(jnp.float32) * attended.astype(jnp.float32), axis=1, keepdims=True))
        dscore_win = (prob_win * (dprob_win - delta)).astype(jnp.bfloat16)
        dscore_pil = (prob_pil * (dprob_pil - delta)).astype(jnp.bfloat16)
        query_grad = (jnp.dot(dscore_win, key_head, preferred_element_type=jnp.float32) + jnp.dot(dscore_pil, pilot_key, preferred_element_type=jnp.float32)) * scaling
        keywin_grad = jnp.dot(dscore_win.T, query_head, preferred_element_type=jnp.float32) * scaling
        valwin_grad = jnp.dot(weight_win.T, grad_head, preferred_element_type=jnp.float32)
        keypil_grad = jnp.dot(dscore_pil.T, query_head, preferred_element_type=jnp.float32) * scaling
        valpil_grad = jnp.dot(weight_pil.T, grad_head, preferred_element_type=jnp.float32)
        return (attended, query_grad, keywin_grad, valwin_grad, keypil_grad, valpil_grad)
    stacked = lax.map(one_head, (split_heads(query_block), split_heads(key_win), split_heads(val_win), split_heads(key_pil), split_heads(val_pil), split_heads(grad_att)))
    return tuple((join_heads(matrix) for matrix in stacked))

def round_iteration(asker_per_round, lookup_per_round, content_per_round, derivative_per_round, result_weight_matrix, reference_comb_shift, symbol_frame_label):
    grad_att = jnp.dot(derivative_per_round, result_weight_matrix.T, preferred_element_type=jnp.float32).astype(jnp.bfloat16)
    slot_width = PIECE_SYMBOLS // PIL_SHARD
    positions = (jnp.arange(N_SEQ, dtype=jnp.int32)[:, None] * PIECE_SYMBOLS + jnp.arange(PIL_SHARD, dtype=jnp.int32)[None, :] * slot_width + reference_comb_shift).astype(jnp.int32)
    frame_pos = positions.reshape(FRAMES, FRAME_PILOTS)
    key_pil_all = lookup_per_round[frame_pos]
    val_pil_all = content_per_round[frame_pos]
    key_pad = jnp.pad(lookup_per_round, ((HALF_SPAN, HALF_SPAN), (0, 0)))
    val_pad = jnp.pad(content_per_round, ((HALF_SPAN, HALF_SPAN), (0, 0)))
    extended_frame_label = jnp.pad(symbol_frame_label, (HALF_SPAN, HALF_SPAN), constant_values=-1)
    neighborhood_breadth = PIECE_SYMBOLS + 2 * HALF_SPAN

    def shard_step(running, current_shard_index):
        keypad_grad, valpad_grad, keypil_sum, valpil_sum, weight_sum = running
        first_line = (current_shard_index * PIECE_SYMBOLS).astype(jnp.int32)
        frame_index = (current_shard_index // FRAME_SHARDS).astype(jnp.int32)
        query_block = lax.dynamic_slice_in_dim(asker_per_round, first_line, PIECE_SYMBOLS, 0)
        grad_block = lax.dynamic_slice_in_dim(derivative_per_round, first_line, PIECE_SYMBOLS, 0)
        att_block = lax.dynamic_slice_in_dim(grad_att, first_line, PIECE_SYMBOLS, 0)
        key_win = lax.dynamic_slice_in_dim(key_pad, first_line, neighborhood_breadth, 0)
        val_win = lax.dynamic_slice_in_dim(val_pad, first_line, neighborhood_breadth, 0)
        local_admit_filter = joint_admit_filter(lax.dynamic_slice_in_dim(extended_frame_label, first_line, neighborhood_breadth, 0), PIECE_SYMBOLS)
        key_pil = lax.dynamic_index_in_dim(key_pil_all, frame_index, 0, keepdims=False)
        val_pil = lax.dynamic_index_in_dim(val_pil_all, frame_index, 0, keepdims=False)
        results = attend_shard(query_block, key_win, val_win, key_pil, val_pil, local_admit_filter, att_block)
        attended, query_grad, keywin_grad, valwin_grad, keypil_grad, valpil_grad = results
        keywin_round = lax.optimization_barrier(keywin_grad.astype(jnp.bfloat16)).astype(jnp.float32)
        valwin_round = lax.optimization_barrier(valwin_grad.astype(jnp.bfloat16)).astype(jnp.float32)
        keypad_grad = lax.dynamic_update_slice_in_dim(keypad_grad, lax.dynamic_slice_in_dim(keypad_grad, first_line, neighborhood_breadth, 0) + keywin_round, first_line, 0)
        valpad_grad = lax.dynamic_update_slice_in_dim(valpad_grad, lax.dynamic_slice_in_dim(valpad_grad, first_line, neighborhood_breadth, 0) + valwin_round, first_line, 0)
        key_round = lax.optimization_barrier(keypil_grad.astype(jnp.bfloat16)).astype(jnp.float32)
        val_round = lax.optimization_barrier(valpil_grad.astype(jnp.bfloat16)).astype(jnp.float32)
        keypil_sum = lax.dynamic_update_index_in_dim(keypil_sum, lax.dynamic_index_in_dim(keypil_sum, frame_index, 0, keepdims=False) + key_round, frame_index, 0)
        valpil_sum = lax.dynamic_update_index_in_dim(valpil_sum, lax.dynamic_index_in_dim(valpil_sum, frame_index, 0, keepdims=False) + val_round, frame_index, 0)
        weight_sum = weight_sum + jnp.dot(attended.T, grad_block, preferred_element_type=jnp.float32)
        mixed_block = jnp.dot(attended, result_weight_matrix, preferred_element_type=jnp.float32).astype(jnp.bfloat16)
        return ((keypad_grad, valpad_grad, keypil_sum, valpil_sum, weight_sum), (mixed_block, query_grad.astype(jnp.bfloat16)))
    initial = (jnp.zeros((ROUND_SYMBOLS + 2 * HALF_SPAN, D), jnp.float32), jnp.zeros((ROUND_SYMBOLS + 2 * HALF_SPAN, D), jnp.float32), jnp.zeros((FRAMES, FRAME_PILOTS, D), jnp.float32), jnp.zeros((FRAMES, FRAME_PILOTS, D), jnp.float32), jnp.zeros((D, D), jnp.float32))
    running, blocks = lax.scan(shard_step, initial, jnp.arange(N_SEQ, dtype=jnp.int32))
    keypad_grad, valpad_grad, keypil_sum, valpil_sum, weight_sum = running
    mixed_blocks, qgrad_blocks = blocks
    flat_pos = frame_pos.reshape(-1)
    key_grad = keypad_grad[HALF_SPAN:HALF_SPAN + ROUND_SYMBOLS].at[flat_pos].add(keypil_sum.reshape(-1, D))
    value_grad = valpad_grad[HALF_SPAN:HALF_SPAN + ROUND_SYMBOLS].at[flat_pos].add(valpil_sum.reshape(-1, D))
    return (mixed_blocks.reshape(ROUND_SYMBOLS, D), qgrad_blocks.reshape(ROUND_SYMBOLS, D), key_grad.astype(jnp.bfloat16), value_grad.astype(jnp.bfloat16), weight_sum)

def reference(mapped_askers, mapped_lookups, mapped_contents, result_cotangent, result_weight_matrix, reference_comb_shift, symbol_frame_label):

    def pass_fn(round_arguments):
        return round_iteration(round_arguments[0], round_arguments[1], round_arguments[2], round_arguments[3], result_weight_matrix, reference_comb_shift, symbol_frame_label)
    mixed, query_grad, key_grad, value_grad, weight_parts = lax.map(pass_fn, (mapped_askers, mapped_lookups, mapped_contents, result_cotangent))
    weight_grad = lax.optimization_barrier(jnp.sum(weight_parts, axis=0)) / math.sqrt(PASSES * ROUND_SYMBOLS)
    return (mixed, query_grad, key_grad, value_grad, weight_grad)
```

```python
import functools
import math

import jax
import jax.numpy as jnp
from jax import lax
from jax.experimental import pallas as pl
from jax.experimental.pallas import tpu as pltpu
from jax.sharding import Mesh, PartitionSpec as P

HEADS = 8
HALF_SPAN = 256
SHARDS = 8
ROWS = 256
HD = 128
PILS = 32
SLOT = ROWS // PILS
FRAME_ROWS = SHARDS * ROWS
BLOCKS = SHARDS + 2
KV_ROWS = 2 * ROWS + PILS
BF = jnp.bfloat16
F32 = jnp.float32

FRAME = ("xl", "y")
FRAMES = ("zh", "xh")
SCALE = 1.0 / math.sqrt(HD)
LOG2E = math.log2(math.e)


def mm(a, b, ca, cb):
    return lax.dot_general(a, b, (((ca,), (cb,)), ((), ())), preferred_element_type=F32)


def pack_kv_kernel(k_ref, v_ref, s_ref, o_ref):
    o_ref[0, :ROWS] = k_ref[...]
    o_ref[0, ROWS : 2 * ROWS] = v_ref[...]
    o_ref[0, 2 * ROWS :] = s_ref[...]


def pack_kv(k, v, shift_cols):
    return pl.pallas_call(
        pack_kv_kernel,
        grid=(HEADS,),
        in_specs=[
            pl.BlockSpec((ROWS, HD), lambda h: (0, h)),
            pl.BlockSpec((ROWS, HD), lambda h: (0, h)),
            pl.BlockSpec((PILS, HD), lambda h: (0, 0)),
        ],
        out_specs=pl.BlockSpec((1, KV_ROWS, HD), lambda h: (h, 0, 0)),
        out_shape=jax.ShapeDtypeStruct((HEADS, KV_ROWS, HD), BF),
        name="pack_kv",
    )(k, v, shift_cols)


def pack_qg_kernel(q_ref, g_ref, w_ref, o_ref):
    o_ref[0, :ROWS] = q_ref[...]
    o_ref[0, ROWS:] = mm(g_ref[...], w_ref[...], 1, 1).astype(BF)


def pack_qg(q, g, w):
    width = g.shape[1]
    return pl.pallas_call(
        pack_qg_kernel,
        grid=(HEADS,),
        in_specs=[
            pl.BlockSpec((ROWS, HD), lambda h: (0, h)),
            pl.BlockSpec((ROWS, width), lambda h: (0, 0)),
            pl.BlockSpec((HD, width), lambda h: (h, 0)),
        ],
        out_specs=pl.BlockSpec((1, 2 * ROWS, HD), lambda h: (h, 0, 0)),
        out_shape=jax.ShapeDtypeStruct((HEADS, 2 * ROWS, HD), BF),
        name="pack_qg",
    )(q, g, w)


def pilot_pick(shift):
    where_to = lax.broadcasted_iota(jnp.int32, (PILS, HD), 0) * SLOT + shift.astype(F32).astype(jnp.int32)
    lane = lax.broadcasted_iota(jnp.int32, (PILS, HD), 1)
    picks = [jnp.where(lane + part * HD == where_to, 1.0, 0.0) for part in range(ROWS // HD)]
    return jnp.concatenate(picks, axis=1).astype(BF)


def attend_kernel(
    kv_ref, qg_ref, left_ref, right_ref, labk_ref, labq_ref,
    att_ref, dq_ref, dkv_ref, dleft_ref, dright_ref,
    k_all, v_all, kt_all, vt_all, k_pil, v_pil, kt_pil, vt_pil, dk_all, dv_all, dk_pil, dv_pil,
):
    i = pl.program_id(0)

    @pl.when(i == 0)
    def _():
        for b in range(BLOCKS):
            if b == 0:
                kb, vb = left_ref[:ROWS], left_ref[ROWS:]
            elif b == BLOCKS - 1:
                kb, vb = right_ref[:ROWS], right_ref[ROWS:]
            else:
                kb, vb = kv_ref[b - 1, :ROWS], kv_ref[b - 1, ROWS : 2 * ROWS]
            k_all[b] = kb
            v_all[b] = vb
            kt_all[b] = kb.T
            vt_all[b] = vb.T
            if 0 < b < BLOCKS - 1:
                pick = pilot_pick(kv_ref[b - 1, 2 * ROWS :])
                at = slice((b - 1) * PILS, b * PILS)
                k_pil[at] = mm(pick, kb, 1, 0).astype(BF)
                v_pil[at] = mm(pick, vb, 1, 0).astype(BF)
        kt_pil[...] = k_pil[...].T
        vt_pil[...] = v_pil[...].T
        dk_all[...] = jnp.zeros_like(dk_all)
        dv_all[...] = jnp.zeros_like(dv_all)
        dk_pil[...] = jnp.zeros_like(dk_pil)
        dv_pil[...] = jnp.zeros_like(dv_pil)

    q = qg_ref[i, :ROWS]
    ga = qg_ref[i, ROWS:]
    label_q = labq_ref[i]
    key_at = lax.broadcasted_iota(jnp.int32, (ROWS, ROWS), 0)
    query_at = lax.broadcasted_iota(jnp.int32, (ROWS, ROWS), 1)
    scores = []
    for part in range(3):
        label_k = labk_ref[i + part][:, :1]
        admit = label_k == label_q
        if part == 0:
            admit = admit & (key_at >= query_at)
        elif part == 2:
            admit = admit & (key_at <= query_at)
        scores.append(jnp.where(admit, mm(k_all[i + part], q, 1, 1), -jnp.inf))
    scores.append(mm(k_pil[...], q, 1, 1))
    top = functools.reduce(jnp.maximum, [jnp.max(s, axis=0, keepdims=True) for s in scores])
    factor = SCALE * LOG2E
    top = top * factor
    exps = [jnp.exp2(s * factor - top) for s in scores]
    inverse = 1.0 / functools.reduce(jnp.add, [jnp.sum(e, axis=0, keepdims=True) for e in exps])
    probs = [e * inverse for e in exps]
    weights = [p.astype(BF) for p in probs]
    vts = [vt_all[i + part] for part in range(3)] + [vt_pil[...]]
    att_t = functools.reduce(jnp.add, [mm(vt, w, 1, 0) for vt, w in zip(vts, weights)])
    att = att_t.T.astype(BF)
    att_ref[i] = att
    product = ga.astype(F32) * att.astype(F32)
    delta = jnp.sum(product.T, axis=0, keepdims=True)
    vals = [v_all[i + part] for part in range(3)] + [v_pil[...]]
    kts = [kt_all[i + part] for part in range(3)] + [kt_pil[...]]
    dq_t = jnp.zeros((HD, ROWS), F32)
    for part in range(4):
        dprob = mm(vals[part], ga, 1, 1)
        dscore = (probs[part] * (dprob - delta)).astype(BF)
        dq_t = dq_t + mm(kts[part], dscore, 1, 0)
        dk = mm(dscore, q, 1, 0)
        dv = mm(weights[part], ga, 1, 0)
        if part < 3:
            dk_all[i + part] += dk
            dv_all[i + part] += dv
        else:
            dk_pil[...] += dk
            dv_pil[...] += dv
    dq_ref[i] = (dq_t * SCALE).T.astype(BF)

    @pl.when(i == SHARDS - 1)
    def _():
        for sh in range(SHARDS):
            pick = pilot_pick(kv_ref[sh, 2 * ROWS :])
            at = slice(sh * PILS, (sh + 1) * PILS)
            for which, (own, pil, by) in enumerate(((dk_all, dk_pil, SCALE), (dv_all, dv_pil, 1.0))):
                fine = pil[at]
                high = fine.astype(BF)
                low = (fine - high.astype(F32)).astype(BF)
                total = own[sh + 1] + (mm(pick, high, 0, 0) + mm(pick, low, 0, 0))
                dkv_ref[sh, which * ROWS : (which + 1) * ROWS] = (total * by).astype(BF)
        for ref, b in ((dleft_ref, 0), (dright_ref, BLOCKS - 1)):
            ref[:ROWS] = (dk_all[b] * SCALE).astype(BF)
            ref[ROWS:] = dv_all[b].astype(BF)


def whole(shape):
    return pl.BlockSpec(shape, lambda i: (0,) * len(shape))


def attend(kv, qg, left, right, labk, labq):
    ins = (kv, qg, left, right, labk, labq)
    outs = [
        (SHARDS, ROWS, HD), (SHARDS, ROWS, HD), (SHARDS, 2 * ROWS, HD), (2 * ROWS, HD), (2 * ROWS, HD),
    ]
    matmul = 2 * FRAME_ROWS * 4 * ROWS * HD
    return pl.pallas_call(
        attend_kernel,
        grid=(SHARDS,),
        in_specs=[whole(a.shape) for a in ins],
        out_specs=[whole(s) for s in outs],
        out_shape=[jax.ShapeDtypeStruct(s, BF) for s in outs],
        scratch_shapes=[
            pltpu.VMEM((BLOCKS, ROWS, HD), BF),
            pltpu.VMEM((BLOCKS, ROWS, HD), BF),
            pltpu.VMEM((BLOCKS, HD, ROWS), BF),
            pltpu.VMEM((BLOCKS, HD, ROWS), BF),
            pltpu.VMEM((SHARDS * PILS, HD), BF),
            pltpu.VMEM((SHARDS * PILS, HD), BF),
            pltpu.VMEM((HD, SHARDS * PILS), BF),
            pltpu.VMEM((HD, SHARDS * PILS), BF),
            pltpu.VMEM((BLOCKS, ROWS, HD), F32),
            pltpu.VMEM((BLOCKS, ROWS, HD), F32),
            pltpu.VMEM((SHARDS * PILS, HD), F32),
            pltpu.VMEM((SHARDS * PILS, HD), F32),
        ],
        compiler_params=pltpu.CompilerParams(vmem_limit_bytes=48 * 1024 * 1024),
        cost_estimate=pl.CostEstimate(
            flops=6 * matmul, bytes_accessed=8 << 20, transcendentals=FRAME_ROWS * 4 * ROWS
        ),
        name="attend",
    )(*ins)


def finish_kernel(att_ref, g_ref, w_ref, mixed_ref, share_ref, acc):
    h = pl.program_id(0)
    att = att_ref[0]
    part = mm(att, w_ref[...], 1, 0)

    @pl.when(h == 0)
    def _():
        acc[...] = part

    @pl.when(h > 0)
    def _():
        acc[...] += part

    share_ref[0] = mm(att, g_ref[...], 0, 0)

    @pl.when(h == HEADS - 1)
    def _():
        mixed_ref[...] = acc[...].astype(BF)


def finish(att, g, w):
    width = g.shape[1]
    return pl.pallas_call(
        finish_kernel,
        grid=(HEADS,),
        in_specs=[
            pl.BlockSpec((1, ROWS, HD), lambda h: (h, 0, 0)),
            pl.BlockSpec((ROWS, width), lambda h: (0, 0)),
            pl.BlockSpec((HD, width), lambda h: (h, 0)),
        ],
        out_specs=[
            pl.BlockSpec((ROWS, width), lambda h: (0, 0)),
            pl.BlockSpec((1, HD, width), lambda h: (h, 0, 0)),
        ],
        out_shape=[
            jax.ShapeDtypeStruct((ROWS, width), BF),
            jax.ShapeDtypeStruct((HEADS, HD, width), F32),
        ],
        scratch_shapes=[pltpu.VMEM((ROWS, width), F32)],
        name="finish",
    )(att, g, w)


def halved(value, dim, axis, bit):
    count = lax.axis_size(axis)
    size = value.shape[dim] // 2
    upper = (lax.axis_index(axis) >> bit) & 1 == 1
    low = lax.slice_in_dim(value, 0, size, axis=dim)
    high = lax.slice_in_dim(value, size, 2 * size, axis=dim)
    out = jnp.where(upper, low, high).astype(BF)
    got = lax.ppermute(out, axis, [(j, j ^ (1 << bit)) for j in range(count)])
    return jnp.where(upper, high, low) + got.astype(F32)


def to_heads(x):
    return lax.all_to_all(x, FRAME, 0, 0, tiled=True)


def joined(x):
    return jnp.transpose(x, (1, 0, 2)).reshape(ROWS, HEADS * HD)


def on_device(askers, lookups, contents, cotangent, w, comb_shift, label):
    q, k, v, g = askers[0], lookups[0], contents[0], cotangent[0]
    frame = lax.axis_index(FRAMES)
    ups = [(j, j + 1) for j in range(lax.axis_size(FRAMES) - 1)]
    downs = [(j, i) for i, j in ups]

    shift_cols = jnp.broadcast_to(comb_shift[0].astype(BF)[:, None], (PILS, HD))
    kv = to_heads(pack_kv(k, v, shift_cols))
    left = lax.ppermute(kv[SHARDS - 1, : 2 * ROWS], FRAMES, ups)
    right = lax.ppermute(kv[0, : 2 * ROWS], FRAMES, downs)
    qg = to_heads(pack_qg(q, g, w))

    label = jnp.pad(label, (HALF_SPAN, HALF_SPAN), constant_values=-1)
    label = lax.dynamic_slice_in_dim(label, frame * FRAME_ROWS, BLOCKS * ROWS, 0)
    labk = jnp.broadcast_to(label.reshape(BLOCKS, ROWS, 1), (BLOCKS, ROWS, HD))
    labq = label[HALF_SPAN : HALF_SPAN + FRAME_ROWS].reshape(SHARDS, 1, ROWS)

    att, dq, dkv, dleft, dright = attend(kv, qg, left, right, labk, labq)

    from_right = lax.ppermute(dleft, FRAMES, downs)
    from_left = lax.ppermute(dright, FRAMES, ups)
    att = to_heads(att)
    mixed, share = finish(att, g, w)

    width = share.shape[-1]
    share = share.reshape(4, 2, HD, width)
    share = halved(share, 1, "c", 0).reshape(4, HD, width)
    share = halved(share, 0, "zl", 1)
    share = halved(share, 0, "zl", 0)[0]
    share = halved(share, 0, "zh", 0)
    share = halved(share, 0, "xh", 0)
    share = halved(share, 0, "xl", 0)
    share = halved(share, 0, "y", 1)
    share = halved(share, 0, "y", 0)
    weight_grad = share * (1.0 / math.sqrt(8 * 32 * ROWS))

    dq = to_heads(dq)
    first = dkv[:1].astype(F32) + from_left.astype(F32)[None]
    last = dkv[SHARDS - 1 :].astype(F32) + from_right.astype(F32)[None]
    dkv = jnp.concatenate([first.astype(BF), dkv[1 : SHARDS - 1], last.astype(BF)], axis=0)
    dkv = to_heads(dkv)
    return (
        mixed[None],
        joined(dq)[None],
        joined(dkv[:, :ROWS])[None],
        joined(dkv[:, ROWS:])[None],
        weight_grad,
    )


def solution(mesh):
    fine = Mesh(mesh.devices.reshape(4, 2, 2, 2, 2, 4), ("zl", "c", "zh", "xh", "xl", "y"))
    dp, seq = ("zl", "c"), ("zh", "xh", "xl", "y")
    rows = P(dp, seq, None)
    return jax.shard_map(
        on_device,
        mesh=fine,
        in_specs=(rows, rows, rows, rows, P(), P(seq, None), P()),
        out_specs=(rows, rows, rows, rows, P(dp + seq, None)),
        check_vma=False,
    )
```

```python
import functools
import math

import jax
import jax.numpy as jnp
from jax import lax
from jax.experimental import pallas as pl
from jax.experimental.pallas import tpu as pltpu
from jax.sharding import Mesh, PartitionSpec as P

HEADS = 8
HALF_SPAN = 256
SHARDS = 8
ROWS = 256
HD = 128
PILS = 32
SLOT = ROWS // PILS
FRAME_ROWS = SHARDS * ROWS
BLOCKS = SHARDS + 2
KV_ROWS = 2 * ROWS + PILS
BF = jnp.bfloat16
F32 = jnp.float32

FRAME = ("xl", "y")
FRAMES = ("zh", "xh")
SCALE = 1.0 / math.sqrt(HD)
LOG2E = math.log2(math.e)


def mm(a, b, ca, cb):
    return lax.dot_general(a, b, (((ca,), (cb,)), ((), ())), preferred_element_type=F32)


def pack_kv_kernel(k_ref, v_ref, s_ref, o_ref):
    for n in range(o_ref.shape[0]):
        columns = slice(n * HD, (n + 1) * HD)
        o_ref[n, :ROWS] = k_ref[:, columns]
        o_ref[n, ROWS : 2 * ROWS] = v_ref[:, columns]
        o_ref[n, 2 * ROWS :] = s_ref[...]


def pack_kv(k, v, shift_cols):
    some = 4
    return pl.pallas_call(
        pack_kv_kernel,
        grid=(HEADS // some,),
        in_specs=[
            pl.BlockSpec((ROWS, some * HD), lambda h: (0, h)),
            pl.BlockSpec((ROWS, some * HD), lambda h: (0, h)),
            pl.BlockSpec((PILS, HD), lambda h: (0, 0)),
        ],
        out_specs=pl.BlockSpec((some, KV_ROWS, HD), lambda h: (h, 0, 0)),
        out_shape=jax.ShapeDtypeStruct((HEADS, KV_ROWS, HD), BF),
        name="pack_kv",
    )(k, v, shift_cols)


def pack_qg_kernel(q_ref, g_ref, w_ref, o_ref):
    grad = mm(g_ref[...], w_ref[...], 1, 1).astype(BF)
    for n in range(o_ref.shape[0]):
        columns = slice(n * HD, (n + 1) * HD)
        o_ref[n, :ROWS] = q_ref[:, columns]
        o_ref[n, ROWS:] = grad[:, columns]


def pack_qg(q, g, w):
    width = g.shape[1]
    some = 2
    return pl.pallas_call(
        pack_qg_kernel,
        grid=(HEADS // some,),
        in_specs=[
            pl.BlockSpec((ROWS, some * HD), lambda h: (0, h)),
            pl.BlockSpec((ROWS, width), lambda h: (0, 0)),
            pl.BlockSpec((some * HD, width), lambda h: (h, 0)),
        ],
        out_specs=pl.BlockSpec((some, 2 * ROWS, HD), lambda h: (h, 0, 0)),
        out_shape=jax.ShapeDtypeStruct((HEADS, 2 * ROWS, HD), BF),
        cost_estimate=pl.CostEstimate(
            flops=2 * ROWS * width * width, bytes_accessed=5 << 20, transcendentals=0
        ),
        name="pack_qg",
    )(q, g, w)


def pilot_pick(shift):
    where_to = lax.broadcasted_iota(jnp.int32, (PILS, HD), 0) * SLOT + shift.astype(F32).astype(jnp.int32)
    lane = lax.broadcasted_iota(jnp.int32, (PILS, HD), 1)
    picks = [jnp.where(lane + part * HD == where_to, 1.0, 0.0) for part in range(ROWS // HD)]
    return jnp.concatenate(picks, axis=1).astype(BF)


def window_scores(i, q, k_all, k_pil, labk_ref, labq_ref):
    label_q = labq_ref[i]
    key_at = lax.broadcasted_iota(jnp.int32, (ROWS, ROWS), 0)
    query_at = lax.broadcasted_iota(jnp.int32, (ROWS, ROWS), 1)
    scores = []
    for part in range(3):
        admit = labk_ref[i + part][:, :1] == label_q
        if part == 0:
            admit = admit & (key_at >= query_at)
        elif part == 2:
            admit = admit & (key_at <= query_at)
        scores.append(jnp.where(admit, mm(k_all[i + part], q, 1, 1), -jnp.inf))
    return scores + [mm(k_pil[...], q, 1, 1)]


def block_of(b, kv_ref, left_ref, right_ref):
    if b == 0:
        return left_ref[:ROWS], left_ref[ROWS:]
    if b == BLOCKS - 1:
        return right_ref[:ROWS], right_ref[ROWS:]
    return kv_ref[b - 1, :ROWS], kv_ref[b - 1, ROWS : 2 * ROWS]


def forward_kernel(
    kv_ref, qg_ref, left_ref, right_ref, labk_ref, labq_ref,
    att_ref, stat_ref, k_pil, v_pil,
    k_all, vt_all, vt_pil,
):
    i = pl.program_id(0)

    @pl.when(i == 0)
    def _():
        for b in range(BLOCKS):
            kb, vb = block_of(b, kv_ref, left_ref, right_ref)
            k_all[b] = kb
            vt_all[b] = vb.T
            if 0 < b < BLOCKS - 1:
                pick = pilot_pick(kv_ref[b - 1, 2 * ROWS :])
                at = slice((b - 1) * PILS, b * PILS)
                k_pil[at] = mm(pick, kb, 1, 0).astype(BF)
                v_pil[at] = mm(pick, vb, 1, 0).astype(BF)
        vt_pil[...] = v_pil[...].T

    scores = window_scores(i, qg_ref[i, :ROWS], k_all, k_pil, labk_ref, labq_ref)
    factor = SCALE * LOG2E
    top = functools.reduce(jnp.maximum, [jnp.max(s, axis=0, keepdims=True) for s in scores])
    top = top * factor
    exps = [jnp.exp2(s * factor - top) for s in scores]
    inverse = 1.0 / functools.reduce(jnp.add, [jnp.sum(e, axis=0, keepdims=True) for e in exps])
    stat_ref[i] = jnp.concatenate([top, inverse], axis=0)
    vts = [vt_all[i + part] for part in range(3)] + [vt_pil[...]]
    att_t = functools.reduce(
        jnp.add, [mm(vt, (e * inverse).astype(BF), 1, 0) for vt, e in zip(vts, exps)]
    )
    att_ref[i] = att_t.T.astype(BF)


def backward_kernel(
    kv_ref, qg_ref, left_ref, right_ref, labk_ref, labq_ref, att_ref, stat_ref, k_pil, v_pil,
    dq_ref, dkv_ref, dleft_ref, dright_ref,
    k_all, v_all, kt_all, kt_pil, dk_all, dv_all, dk_pil, dv_pil,
):
    i = pl.program_id(0)

    @pl.when(i == 0)
    def _():
        for b in range(BLOCKS):
            kb, vb = block_of(b, kv_ref, left_ref, right_ref)
            k_all[b] = kb
            v_all[b] = vb
            kt_all[b] = kb.T
        kt_pil[...] = k_pil[...].T
        dk_all[...] = jnp.zeros_like(dk_all)
        dv_all[...] = jnp.zeros_like(dv_all)
        dk_pil[...] = jnp.zeros_like(dk_pil)
        dv_pil[...] = jnp.zeros_like(dv_pil)

    q = qg_ref[i, :ROWS]
    ga = qg_ref[i, ROWS:]
    scores = window_scores(i, q, k_all, k_pil, labk_ref, labq_ref)
    top, inverse = stat_ref[i][:1], stat_ref[i][1:]
    product = ga.astype(F32) * att_ref[i].astype(F32)
    delta = jnp.sum(product.T, axis=0, keepdims=True)
    vals = [v_all[i + part] for part in range(3)] + [v_pil[...]]
    kts = [kt_all[i + part] for part in range(3)] + [kt_pil[...]]
    dq_t = jnp.zeros((HD, ROWS), F32)
    for part in range(4):
        prob = jnp.exp2(scores[part] * (SCALE * LOG2E) - top) * inverse
        dprob = mm(vals[part], ga, 1, 1)
        dscore = (prob * (dprob - delta)).astype(BF)
        dq_t = dq_t + mm(kts[part], dscore, 1, 0)
        dk = mm(dscore, q, 1, 0)
        dv = mm(prob.astype(BF), ga, 1, 0)
        if part < 3:
            dk_all[i + part] += dk
            dv_all[i + part] += dv
        else:
            dk_pil[...] += dk
            dv_pil[...] += dv
    dq_ref[i] = (dq_t * SCALE).T.astype(BF)

    @pl.when(i == SHARDS - 1)
    def _():
        for sh in range(SHARDS):
            pick = pilot_pick(kv_ref[sh, 2 * ROWS :])
            at = slice(sh * PILS, (sh + 1) * PILS)
            for which, (own, pil, by) in enumerate(((dk_all, dk_pil, SCALE), (dv_all, dv_pil, 1.0))):
                fine = pil[at]
                high = fine.astype(BF)
                low = (fine - high.astype(F32)).astype(BF)
                total = own[sh + 1] + (mm(pick, high, 0, 0) + mm(pick, low, 0, 0))
                dkv_ref[sh, which * ROWS : (which + 1) * ROWS] = (total * by).astype(BF)
        for ref, b in ((dleft_ref, 0), (dright_ref, BLOCKS - 1)):
            ref[:ROWS] = (dk_all[b] * SCALE).astype(BF)
            ref[ROWS:] = dv_all[b].astype(BF)


def whole(shape):
    return pl.BlockSpec(shape, lambda i: (0,) * len(shape))


def over_blocks(kernel, name, ins, outs, scratch, matmuls):
    return pl.pallas_call(
        kernel,
        grid=(SHARDS,),
        in_specs=[whole(a.shape) for a in ins],
        out_specs=[whole(o.shape) for o in outs],
        out_shape=outs,
        scratch_shapes=scratch,
        compiler_params=pltpu.CompilerParams(vmem_limit_bytes=48 * 1024 * 1024),
        cost_estimate=pl.CostEstimate(
            flops=matmuls * 2 * FRAME_ROWS * 4 * ROWS * HD,
            bytes_accessed=8 << 20,
            transcendentals=FRAME_ROWS * 4 * ROWS,
        ),
        name=name,
    )(*ins)


def like(*shape, dtype=BF):
    return jax.ShapeDtypeStruct(shape, dtype)


def forward(ins):
    outs = [like(SHARDS, ROWS, HD), like(SHARDS, 2, ROWS, dtype=F32)]
    outs += [like(SHARDS * PILS, HD)] * 2
    scratch = [
        pltpu.VMEM((BLOCKS, ROWS, HD), BF),
        pltpu.VMEM((BLOCKS, HD, ROWS), BF),
        pltpu.VMEM((HD, SHARDS * PILS), BF),
    ]
    return over_blocks(forward_kernel, "forward", ins, outs, scratch, 2)


def backward(ins):
    outs = [like(SHARDS, ROWS, HD), like(SHARDS, 2 * ROWS, HD)] + [like(2 * ROWS, HD)] * 2
    scratch = [
        pltpu.VMEM((BLOCKS, ROWS, HD), BF),
        pltpu.VMEM((BLOCKS, ROWS, HD), BF),
        pltpu.VMEM((BLOCKS, HD, ROWS), BF),
        pltpu.VMEM((HD, SHARDS * PILS), BF),
        pltpu.VMEM((BLOCKS, ROWS, HD), F32),
        pltpu.VMEM((BLOCKS, ROWS, HD), F32),
        pltpu.VMEM((SHARDS * PILS, HD), F32),
        pltpu.VMEM((SHARDS * PILS, HD), F32),
    ]
    return over_blocks(backward_kernel, "backward", ins, outs, scratch, 5)


def mix_kernel(att_ref, w_ref, mixed_ref):
    att = jnp.concatenate([att_ref[h] for h in range(HEADS)], axis=1)
    mixed_ref[...] = mm(att, w_ref[...], 1, 0).astype(BF)


def mix(att, w):
    width = w.shape[1]
    return pl.pallas_call(
        mix_kernel,
        grid=(4,),
        in_specs=[whole(att.shape), pl.BlockSpec((width, width // 4), lambda n: (0, n))],
        out_specs=pl.BlockSpec((ROWS, width // 4), lambda n: (0, n)),
        out_shape=like(ROWS, width),
        cost_estimate=pl.CostEstimate(
            flops=2 * ROWS * width * width, bytes_accessed=3 << 20, transcendentals=0
        ),
        name="mix",
    )(att, w)


def share_kernel(heads_ref, att_ref, g_ref, *refs):
    total = mm(att_ref[0], g_ref[...], 0, 0)
    if len(refs) == 2:
        total = total + refs[0][0].astype(F32)
    refs[-1][0] = total.astype(refs[-1].dtype)


def share_of(att, g, heads, got, dtype):
    width, count = g.shape[1], heads.shape[0]
    block = (1, HD, width)
    in_specs = [
        pl.BlockSpec((1, ROWS, HD), lambda n, heads: (heads[n], 0, 0)),
        pl.BlockSpec((ROWS, width), lambda n, heads: (0, 0)),
    ]
    ins = [heads, att, g]
    if got is not None:
        in_specs.append(pl.BlockSpec(block, lambda n, heads: (heads[n] // 2, 0, 0)))
        ins.append(got)
    return pl.pallas_call(
        share_kernel,
        grid_spec=pltpu.PrefetchScalarGridSpec(
            num_scalar_prefetch=1,
            grid=(count,),
            in_specs=in_specs,
            out_specs=pl.BlockSpec(block, lambda n, heads: (n, 0, 0)),
        ),
        out_shape=like(count, HD, width, dtype=dtype),
        cost_estimate=pl.CostEstimate(
            flops=2 * count * ROWS * HD * width, bytes_accessed=2 << 20, transcendentals=0
        ),
        name="share",
    )(*ins)


def halved(value, dim, axis, bit):
    count = lax.axis_size(axis)
    size = value.shape[dim] // 2
    upper = (lax.axis_index(axis) >> bit) & 1 == 1
    low = lax.slice_in_dim(value, 0, size, axis=dim)
    high = lax.slice_in_dim(value, size, 2 * size, axis=dim)
    out = jnp.where(upper, low, high).astype(BF)
    got = lax.ppermute(out, axis, [(j, j ^ (1 << bit)) for j in range(count)])
    return jnp.where(upper, high, low) + got.astype(F32)


def to_heads(x):
    return lax.all_to_all(x, FRAME, 0, 0, tiled=True)


def joined(x):
    return jnp.transpose(x, (1, 0, 2)).reshape(ROWS, HEADS * HD)


def on_device(askers, lookups, contents, cotangent, w, comb_shift, label):
    q, k, v, g = askers[0], lookups[0], contents[0], cotangent[0]
    frame = lax.axis_index(FRAMES)
    ups = [(j, j + 1) for j in range(lax.axis_size(FRAMES) - 1)]
    downs = [(j, i) for i, j in ups]

    shift_cols = jnp.broadcast_to(comb_shift[0].astype(BF)[:, None], (PILS, HD))
    kv = to_heads(pack_kv(k, v, shift_cols))
    left = lax.ppermute(kv[SHARDS - 1, : 2 * ROWS], FRAMES, ups)
    right = lax.ppermute(kv[0, : 2 * ROWS], FRAMES, downs)
    qg = to_heads(pack_qg(q, g, w))

    label = jnp.pad(label, (HALF_SPAN, HALF_SPAN), constant_values=-1)
    label = lax.dynamic_slice_in_dim(label, frame * FRAME_ROWS, BLOCKS * ROWS, 0)
    labk = jnp.broadcast_to(label.reshape(BLOCKS, ROWS, 1), (BLOCKS, ROWS, HD))
    labq = label[HALF_SPAN : HALF_SPAN + FRAME_ROWS].reshape(SHARDS, 1, ROWS)

    frame_ins = (kv, qg, left, right, labk, labq)
    att, stats, k_pil, v_pil = forward(frame_ins)
    att_rows = to_heads(att)
    dq, dkv, dleft, dright = backward(frame_ins + (att, stats, k_pil, v_pil))
    from_right = lax.ppermute(dleft, FRAMES, downs)
    from_left = lax.ppermute(dright, FRAMES, ups)

    core, z_bit = lax.axis_index("c"), lax.axis_index("zl") & 1
    head = jnp.arange(4, dtype=jnp.int32) * 2
    share = share_of(att_rows, g, head + (1 - core), None, BF)
    got = lax.ppermute(share, "c", [(0, 1), (1, 0)])
    mixed = mix(att_rows, w)
    mine = jnp.arange(2, dtype=jnp.int32) * 4 + core
    send = share_of(att_rows, g, mine + 2 * (1 - z_bit), got, BF)
    keep = share_of(att_rows, g, mine + 2 * z_bit, got, F32)
    got = lax.ppermute(send, "zl", [(j, j ^ 1) for j in range(4)])
    share = keep + got.astype(F32)

    dq = to_heads(dq)
    first = dkv[:1].astype(F32) + from_left.astype(F32)[None]
    last = dkv[SHARDS - 1 :].astype(F32) + from_right.astype(F32)[None]
    dkv = jnp.concatenate([first.astype(BF), dkv[1 : SHARDS - 1], last.astype(BF)], axis=0)
    share = halved(share, 0, "zl", 1)[0]
    share, dq = lax.optimization_barrier((share, dq))
    dkv = to_heads(dkv)

    width = share.shape[-1]
    share = halved(share.reshape(4, 2, 16, width), 1, "xl", 0)
    share = halved(share.reshape(2, 2, 16, width), 1, "xh", 0)
    share = halved(share.reshape(2, 16, width), 0, "zh", 0)
    share = share.reshape(16, width)
    share = halved(share, 0, "y", 1)
    share = halved(share, 0, "y", 0)
    weight_grad = share * (1.0 / math.sqrt(8 * 32 * ROWS))
    return (
        mixed[None],
        joined(dq)[None],
        joined(dkv[:, :ROWS])[None],
        joined(dkv[:, ROWS:])[None],
        weight_grad,
    )


def solution(mesh):
    fine = Mesh(mesh.devices.reshape(4, 2, 2, 2, 2, 4), ("zl", "c", "zh", "xh", "xl", "y"))
    dp, seq = ("zl", "c"), ("zh", "xh", "xl", "y")
    rows = P(dp, seq, None)
    return jax.shard_map(
        on_device,
        mesh=fine,
        in_specs=(rows, rows, rows, rows, P(), P(seq, None), P()),
        out_specs=(rows, rows, rows, rows, P(dp + seq, None)),
        check_vma=False,
    )
```

```python
import functools
import math

import jax
import jax.numpy as jnp
from jax import lax
from jax.experimental import pallas as pl
from jax.experimental.pallas import tpu as pltpu
from jax.sharding import Mesh, PartitionSpec as P

HEADS = 8
HALF_SPAN = 256
SHARDS = 8
ROWS = 256
HD = 128
PILS = 32
SLOT = ROWS // PILS
FRAME_ROWS = SHARDS * ROWS
BLOCKS = SHARDS + 2
KV_ROWS = 2 * ROWS + PILS
BF = jnp.bfloat16
F32 = jnp.float32

FRAME = ("xl", "y")
FRAMES = ("zh", "xh")
SCALE = 1.0 / math.sqrt(HD)
LOG2E = math.log2(math.e)


def mm(a, b, ca, cb):
    return lax.dot_general(a, b, (((ca,), (cb,)), ((), ())), preferred_element_type=F32)


def pack_kv_kernel(k_ref, v_ref, s_ref, o_ref):
    down = lax.broadcasted_iota(jnp.int32, (PILS, PILS), 0)
    along = lax.broadcasted_iota(jnp.int32, (PILS, PILS), 1)
    shift = jnp.where(down == along, s_ref[...].astype(F32), 0.0)
    shift = jnp.broadcast_to(jnp.sum(shift, axis=1, keepdims=True), (PILS, HD)).astype(BF)
    for n in range(o_ref.shape[0]):
        columns = slice(n * HD, (n + 1) * HD)
        o_ref[n, :ROWS] = k_ref[:, columns]
        o_ref[n, ROWS : 2 * ROWS] = v_ref[:, columns]
        o_ref[n, 2 * ROWS :] = shift


def pack_kv(k, v, comb_shift):
    some = 4
    return pl.pallas_call(
        pack_kv_kernel,
        grid=(HEADS // some,),
        in_specs=[
            pl.BlockSpec((ROWS, some * HD), lambda h: (0, h)),
            pl.BlockSpec((ROWS, some * HD), lambda h: (0, h)),
            pl.BlockSpec((1, PILS), lambda h: (0, 0)),
        ],
        out_specs=pl.BlockSpec((some, KV_ROWS, HD), lambda h: (h, 0, 0)),
        out_shape=jax.ShapeDtypeStruct((HEADS, KV_ROWS, HD), BF),
        name="pack_kv",
    )(k, v, comb_shift)


def pack_qg_kernel(q_ref, g_ref, w_ref, qo_ref, go_ref):
    grad = mm(g_ref[...], w_ref[...], 1, 1).astype(BF)
    for n in range(qo_ref.shape[0]):
        columns = slice(n * HD, (n + 1) * HD)
        qo_ref[n] = q_ref[:, columns]
        go_ref[n] = grad[:, columns]


def pack_qg(q, g, w):
    width = g.shape[1]
    some = 2
    return pl.pallas_call(
        pack_qg_kernel,
        grid=(HEADS // some,),
        in_specs=[
            pl.BlockSpec((ROWS, some * HD), lambda h: (0, h)),
            pl.BlockSpec((ROWS, width), lambda h: (0, 0)),
            pl.BlockSpec((some * HD, width), lambda h: (h, 0)),
        ],
        out_specs=[pl.BlockSpec((some, ROWS, HD), lambda h: (h, 0, 0))] * 2,
        out_shape=[jax.ShapeDtypeStruct((HEADS, ROWS, HD), BF)] * 2,
        cost_estimate=pl.CostEstimate(
            flops=2 * ROWS * width * width, bytes_accessed=5 << 20, transcendentals=0
        ),
        name="pack_qg",
    )(q, g, w)


def pilot_pick(shift):
    where_to = lax.broadcasted_iota(jnp.int32, (PILS, HD), 0) * SLOT + shift.astype(F32).astype(jnp.int32)
    lane = lax.broadcasted_iota(jnp.int32, (PILS, HD), 1)
    picks = [jnp.where(lane + part * HD == where_to, 1.0, 0.0) for part in range(ROWS // HD)]
    return jnp.concatenate(picks, axis=1).astype(BF)


def window_scores(i, q, k_all, k_pil, labk_ref, labq_ref):
    label_q = labq_ref[i]
    key_at = lax.broadcasted_iota(jnp.int32, (ROWS, ROWS), 0)
    query_at = lax.broadcasted_iota(jnp.int32, (ROWS, ROWS), 1)
    scores = []
    for part in range(3):
        admit = labk_ref[i + part][:, :1] == label_q
        if part == 0:
            admit = admit & (key_at >= query_at)
        elif part == 2:
            admit = admit & (key_at <= query_at)
        scores.append(jnp.where(admit, mm(k_all[i + part], q, 1, 1), -jnp.inf))
    return scores + [mm(k_pil[...], q, 1, 1)]


def block_of(b, kv_ref, left_ref, right_ref):
    if b == 0:
        return left_ref[:ROWS], left_ref[ROWS:]
    if b == BLOCKS - 1:
        return right_ref[:ROWS], right_ref[ROWS:]
    return kv_ref[b - 1, :ROWS], kv_ref[b - 1, ROWS : 2 * ROWS]


def forward_kernel(
    kv_ref, q_ref, left_ref, right_ref, labk_ref, labq_ref,
    att_ref, stat_ref, k_pil, v_pil,
    k_all, vt_all, vt_pil,
):
    i = pl.program_id(0)

    @pl.when(i == 0)
    def _():
        for b in range(BLOCKS):
            kb, vb = block_of(b, kv_ref, left_ref, right_ref)
            k_all[b] = kb
            vt_all[b] = vb.T
            if 0 < b < BLOCKS - 1:
                pick = pilot_pick(kv_ref[b - 1, 2 * ROWS :])
                at = slice((b - 1) * PILS, b * PILS)
                k_pil[at] = mm(pick, kb, 1, 0).astype(BF)
                v_pil[at] = mm(pick, vb, 1, 0).astype(BF)
        vt_pil[...] = v_pil[...].T

    scores = window_scores(i, q_ref[i], k_all, k_pil, labk_ref, labq_ref)
    factor = SCALE * LOG2E
    top = functools.reduce(jnp.maximum, [jnp.max(s, axis=0, keepdims=True) for s in scores])
    top = top * factor
    exps = [jnp.exp2(s * factor - top) for s in scores]
    inverse = 1.0 / functools.reduce(jnp.add, [jnp.sum(e, axis=0, keepdims=True) for e in exps])
    stat_ref[i] = jnp.concatenate([top, inverse], axis=0)
    vts = [vt_all[i + part] for part in range(3)] + [vt_pil[...]]
    att_t = functools.reduce(
        jnp.add, [mm(vt, (e * inverse).astype(BF), 1, 0) for vt, e in zip(vts, exps)]
    )
    att_ref[i] = att_t.T.astype(BF)


def backward_kernel(
    kv_ref, q_ref, left_ref, right_ref, labk_ref, labq_ref, ga_ref, att_ref, stat_ref, k_pil, v_pil,
    dq_ref, dkv_ref, dleft_ref, dright_ref,
    k_all, v_all, kt_all, kt_pil, dk_all, dv_all, dk_pil, dv_pil,
):
    i = pl.program_id(0)

    @pl.when(i == 0)
    def _():
        for b in range(BLOCKS):
            kb, vb = block_of(b, kv_ref, left_ref, right_ref)
            k_all[b] = kb
            v_all[b] = vb
            kt_all[b] = kb.T
        kt_pil[...] = k_pil[...].T
        dk_all[...] = jnp.zeros_like(dk_all)
        dv_all[...] = jnp.zeros_like(dv_all)
        dk_pil[...] = jnp.zeros_like(dk_pil)
        dv_pil[...] = jnp.zeros_like(dv_pil)

    q = q_ref[i]
    ga = ga_ref[i]
    scores = window_scores(i, q, k_all, k_pil, labk_ref, labq_ref)
    top, inverse = stat_ref[i][:1], stat_ref[i][1:]
    product = ga.astype(F32) * att_ref[i].astype(F32)
    delta = jnp.sum(product.T, axis=0, keepdims=True)
    vals = [v_all[i + part] for part in range(3)] + [v_pil[...]]
    kts = [kt_all[i + part] for part in range(3)] + [kt_pil[...]]
    dq_t = jnp.zeros((HD, ROWS), F32)
    for part in range(4):
        prob = jnp.exp2(scores[part] * (SCALE * LOG2E) - top) * inverse
        dprob = mm(vals[part], ga, 1, 1)
        dscore = (prob * (dprob - delta)).astype(BF)
        dq_t = dq_t + mm(kts[part], dscore, 1, 0)
        dk = mm(dscore, q, 1, 0)
        dv = mm(prob.astype(BF), ga, 1, 0)
        if part < 3:
            dk_all[i + part] += dk
            dv_all[i + part] += dv
        else:
            dk_pil[...] += dk
            dv_pil[...] += dv
    dq_ref[i] = (dq_t * SCALE).T.astype(BF)

    @pl.when(i == SHARDS - 1)
    def _():
        for sh in range(SHARDS):
            pick = pilot_pick(kv_ref[sh, 2 * ROWS :])
            at = slice(sh * PILS, (sh + 1) * PILS)
            for which, (own, pil, by) in enumerate(((dk_all, dk_pil, SCALE), (dv_all, dv_pil, 1.0))):
                fine = pil[at]
                high = fine.astype(BF)
                low = (fine - high.astype(F32)).astype(BF)
                total = own[sh + 1] + (mm(pick, high, 0, 0) + mm(pick, low, 0, 0))
                dkv_ref[sh, which * ROWS : (which + 1) * ROWS] = (total * by).astype(BF)
        for ref, b in ((dleft_ref, 0), (dright_ref, BLOCKS - 1)):
            ref[:ROWS] = (dk_all[b] * SCALE).astype(BF)
            ref[ROWS:] = dv_all[b].astype(BF)


def whole(shape):
    return pl.BlockSpec(shape, lambda i: (0,) * len(shape))


def over_blocks(kernel, name, ins, outs, scratch, matmuls):
    return pl.pallas_call(
        kernel,
        grid=(SHARDS,),
        in_specs=[whole(a.shape) for a in ins],
        out_specs=[whole(o.shape) for o in outs],
        out_shape=outs,
        scratch_shapes=scratch,
        compiler_params=pltpu.CompilerParams(vmem_limit_bytes=48 * 1024 * 1024),
        cost_estimate=pl.CostEstimate(
            flops=matmuls * 2 * FRAME_ROWS * 4 * ROWS * HD,
            bytes_accessed=8 << 20,
            transcendentals=FRAME_ROWS * 4 * ROWS,
        ),
        name=name,
    )(*ins)


def like(*shape, dtype=BF):
    return jax.ShapeDtypeStruct(shape, dtype)


def forward(ins):
    outs = [like(SHARDS, ROWS, HD), like(SHARDS, 2, ROWS, dtype=F32)]
    outs += [like(SHARDS * PILS, HD)] * 2
    scratch = [
        pltpu.VMEM((BLOCKS, ROWS, HD), BF),
        pltpu.VMEM((BLOCKS, HD, ROWS), BF),
        pltpu.VMEM((HD, SHARDS * PILS), BF),
    ]
    return over_blocks(forward_kernel, "forward", ins, outs, scratch, 2)


def backward(ins):
    outs = [like(SHARDS, ROWS, HD), like(SHARDS, 2 * ROWS, HD)] + [like(2 * ROWS, HD)] * 2
    scratch = [
        pltpu.VMEM((BLOCKS, ROWS, HD), BF),
        pltpu.VMEM((BLOCKS, ROWS, HD), BF),
        pltpu.VMEM((BLOCKS, HD, ROWS), BF),
        pltpu.VMEM((HD, SHARDS * PILS), BF),
        pltpu.VMEM((BLOCKS, ROWS, HD), F32),
        pltpu.VMEM((BLOCKS, ROWS, HD), F32),
        pltpu.VMEM((SHARDS * PILS, HD), F32),
        pltpu.VMEM((SHARDS * PILS, HD), F32),
    ]
    return over_blocks(backward_kernel, "backward", ins, outs, scratch, 5)


def mix_kernel(att_ref, w_ref, mixed_ref):
    att = jnp.concatenate([att_ref[h] for h in range(HEADS)], axis=1)
    mixed_ref[...] = mm(att, w_ref[...], 1, 0).astype(BF)


def mix(att, w):
    width = w.shape[1]
    return pl.pallas_call(
        mix_kernel,
        grid=(4,),
        in_specs=[whole(att.shape), pl.BlockSpec((width, width // 4), lambda n: (0, n))],
        out_specs=pl.BlockSpec((ROWS, width // 4), lambda n: (0, n)),
        out_shape=like(ROWS, width),
        cost_estimate=pl.CostEstimate(
            flops=2 * ROWS * width * width, bytes_accessed=3 << 20, transcendentals=0
        ),
        name="mix",
    )(att, w)


def share_kernel(heads_ref, att_ref, g_ref, *refs):
    total = mm(att_ref[0], g_ref[...], 0, 0)
    if len(refs) == 2:
        total = total + refs[0][0].astype(F32)
    refs[-1][0] = total.astype(refs[-1].dtype)


def share_of(att, g, heads, got, dtype):
    width, count = g.shape[1], heads.shape[0]
    block = (1, HD, width)
    in_specs = [
        pl.BlockSpec((1, ROWS, HD), lambda n, heads: (heads[n], 0, 0)),
        pl.BlockSpec((ROWS, width), lambda n, heads: (0, 0)),
    ]
    ins = [heads, att, g]
    if got is not None:
        in_specs.append(pl.BlockSpec(block, lambda n, heads: (heads[n] // 2, 0, 0)))
        ins.append(got)
    return pl.pallas_call(
        share_kernel,
        grid_spec=pltpu.PrefetchScalarGridSpec(
            num_scalar_prefetch=1,
            grid=(count,),
            in_specs=in_specs,
            out_specs=pl.BlockSpec(block, lambda n, heads: (n, 0, 0)),
        ),
        out_shape=like(count, HD, width, dtype=dtype),
        cost_estimate=pl.CostEstimate(
            flops=2 * count * ROWS * HD * width, bytes_accessed=2 << 20, transcendentals=0
        ),
        name="share",
    )(*ins)


def halved(value, dim, axis, bit):
    count = lax.axis_size(axis)
    size = value.shape[dim] // 2
    upper = (lax.axis_index(axis) >> bit) & 1 == 1
    low = lax.slice_in_dim(value, 0, size, axis=dim)
    high = lax.slice_in_dim(value, size, 2 * size, axis=dim)
    out = jnp.where(upper, low, high).astype(BF)
    got = lax.ppermute(out, axis, [(j, j ^ (1 << bit)) for j in range(count)])
    return jnp.where(upper, high, low) + got.astype(F32)


def scattered(value, dim, axes):
    count = lax.axis_size(axes)
    me = lax.axis_index(axes)

    def part(at):
        return lax.dynamic_index_in_dim(value, at, dim, keepdims=False)

    total = part(me)
    for apart in range(1, count):
        out = part(me ^ apart).astype(BF)
        total = total + lax.ppermute(out, axes, [(j, j ^ apart) for j in range(count)]).astype(F32)
    return total


def to_heads(x):
    return lax.all_to_all(x, FRAME, 0, 0, tiled=True)


def joined(x):
    return jnp.transpose(x, (1, 0, 2)).reshape(ROWS, HEADS * HD)


def on_device(askers, lookups, contents, cotangent, w, comb_shift, label):
    q, k, v, g = askers[0], lookups[0], contents[0], cotangent[0]
    frame = lax.axis_index(FRAMES)
    ups = [(j, j + 1) for j in range(lax.axis_size(FRAMES) - 1)]
    downs = [(j, i) for i, j in ups]

    kv = to_heads(pack_kv(k, v, comb_shift))
    left = lax.ppermute(kv[SHARDS - 1, : 2 * ROWS], FRAMES, ups)
    right = lax.ppermute(kv[0, : 2 * ROWS], FRAMES, downs)
    q, ga = pack_qg(q, g, w)
    q, kv = lax.optimization_barrier((q, kv))
    q = to_heads(q)
    q, ga = lax.optimization_barrier((q, ga))

    label = jnp.pad(label, (HALF_SPAN, HALF_SPAN), constant_values=-1)
    label = lax.dynamic_slice_in_dim(label, frame * FRAME_ROWS, BLOCKS * ROWS, 0)
    labk = jnp.broadcast_to(label.reshape(BLOCKS, ROWS, 1), (BLOCKS, ROWS, HD))
    labq = label[HALF_SPAN : HALF_SPAN + FRAME_ROWS].reshape(SHARDS, 1, ROWS)

    frame_ins = (kv, q, left, right, labk, labq)
    att, stats, k_pil, v_pil = forward(frame_ins)
    ga = to_heads(ga)
    att_rows = to_heads(att)
    dq, dkv, dleft, dright = backward(frame_ins + (ga, att, stats, k_pil, v_pil))
    att_rows, dq, dkv, dleft, dright = lax.optimization_barrier((att_rows, dq, dkv, dleft, dright))
    from_right = lax.ppermute(dleft, FRAMES, downs)
    from_left = lax.ppermute(dright, FRAMES, ups)

    core, z_bit = lax.axis_index("c"), lax.axis_index("zl") & 1
    head = jnp.arange(4, dtype=jnp.int32) * 2
    share = share_of(att_rows, g, head + (1 - core), None, BF)
    got = lax.ppermute(share, "c", [(0, 1), (1, 0)])
    mine = jnp.arange(2, dtype=jnp.int32) * 4 + core
    send = share_of(att_rows, g, mine + 2 * (1 - z_bit), got, BF)
    send, from_left, from_right = lax.optimization_barrier((send, from_left, from_right))
    keep = share_of(att_rows, g, mine + 2 * z_bit, got, F32)
    got = lax.ppermute(send, "zl", [(j, j ^ 1) for j in range(4)])
    share = keep + got.astype(F32)

    dq = to_heads(dq)
    first = dkv[:1].astype(F32) + from_left.astype(F32)[None]
    last = dkv[SHARDS - 1 :].astype(F32) + from_right.astype(F32)[None]
    dkv = jnp.concatenate([first.astype(BF), dkv[1 : SHARDS - 1], last.astype(BF)], axis=0)
    share, dq, dkv = lax.optimization_barrier((share, dq, dkv))
    dkv = to_heads(dkv)
    mixed = mix(att_rows, w)
    share = halved(share, 0, "zl", 1)[0]
    share, dkv, mixed = lax.optimization_barrier((share, dkv, mixed))

    width = share.shape[-1]
    share = scattered(share.reshape(2, 4, 16, width), 1, ("xh", "xl"))
    share = halved(share, 0, "zh", 0)
    share = scattered(share.reshape(4, 4, width), 0, ("y",))
    weight_grad = share * (1.0 / math.sqrt(8 * 32 * ROWS))
    return (
        mixed[None],
        joined(dq)[None],
        joined(dkv[:, :ROWS])[None],
        joined(dkv[:, ROWS:])[None],
        weight_grad,
    )


def solution(mesh):
    fine = Mesh(mesh.devices.reshape(4, 2, 2, 2, 2, 4), ("zl", "c", "zh", "xh", "xl", "y"))
    dp, seq = ("zl", "c"), ("zh", "xh", "xl", "y")
    rows = P(dp, seq, None)
    return jax.shard_map(
        on_device,
        mesh=fine,
        in_specs=(rows, rows, rows, rows, P(), P(seq, None), P()),
        out_specs=(rows, rows, rows, rows, P(dp + seq, None)),
        check_vma=False,
    )
```

```python
import functools
import math

import jax
import jax.numpy as jnp
from jax import lax
from jax.experimental import pallas as pl
from jax.experimental.pallas import tpu as pltpu
from jax.sharding import Mesh, PartitionSpec as P

HEADS = 8
HALF_SPAN = 256
SHARDS = 8
ROWS = 256
HD = 128
PILS = 32
SLOT = ROWS // PILS
FRAME_ROWS = SHARDS * ROWS
BLOCKS = SHARDS + 2
KV_ROWS = 2 * ROWS + PILS
BF = jnp.bfloat16
F32 = jnp.float32

FRAME = ("xl", "y")
FRAMES = ("zh", "xh")
SCALE = 1.0 / math.sqrt(HD)
LOG2E = math.log2(math.e)


def mm(a, b, ca, cb):
    return lax.dot_general(a, b, (((ca,), (cb,)), ((), ())), preferred_element_type=F32)


def pack_kv_kernel(k_ref, v_ref, s_ref, o_ref):
    down = lax.broadcasted_iota(jnp.int32, (PILS, PILS), 0)
    along = lax.broadcasted_iota(jnp.int32, (PILS, PILS), 1)
    shift = jnp.where(down == along, s_ref[...].astype(F32), 0.0)
    shift = jnp.broadcast_to(jnp.sum(shift, axis=1, keepdims=True), (PILS, HD)).astype(BF)
    for n in range(o_ref.shape[0]):
        columns = slice(n * HD, (n + 1) * HD)
        o_ref[n, :ROWS] = k_ref[:, columns]
        o_ref[n, ROWS : 2 * ROWS] = v_ref[:, columns]
        o_ref[n, 2 * ROWS :] = shift


def pack_kv(k, v, comb_shift):
    some = 4
    return pl.pallas_call(
        pack_kv_kernel,
        grid=(HEADS // some,),
        in_specs=[
            pl.BlockSpec((ROWS, some * HD), lambda h: (0, h)),
            pl.BlockSpec((ROWS, some * HD), lambda h: (0, h)),
            pl.BlockSpec((1, PILS), lambda h: (0, 0)),
        ],
        out_specs=pl.BlockSpec((some, KV_ROWS, HD), lambda h: (h, 0, 0)),
        out_shape=jax.ShapeDtypeStruct((HEADS, KV_ROWS, HD), BF),
        name="pack_kv",
    )(k, v, comb_shift)


def pack_qg_kernel(q_ref, g_ref, w_ref, qo_ref, go_ref):
    grad = mm(g_ref[...], w_ref[...], 1, 1).astype(BF)
    for n in range(qo_ref.shape[0]):
        columns = slice(n * HD, (n + 1) * HD)
        qo_ref[n] = q_ref[:, columns]
        go_ref[n] = grad[:, columns]


def pack_qg(q, g, w):
    width = g.shape[1]
    some = 2
    return pl.pallas_call(
        pack_qg_kernel,
        grid=(HEADS // some,),
        in_specs=[
            pl.BlockSpec((ROWS, some * HD), lambda h: (0, h)),
            pl.BlockSpec((ROWS, width), lambda h: (0, 0)),
            pl.BlockSpec((some * HD, width), lambda h: (h, 0)),
        ],
        out_specs=[pl.BlockSpec((some, ROWS, HD), lambda h: (h, 0, 0))] * 2,
        out_shape=[jax.ShapeDtypeStruct((HEADS, ROWS, HD), BF)] * 2,
        cost_estimate=pl.CostEstimate(
            flops=2 * ROWS * width * width, bytes_accessed=5 << 20, transcendentals=0
        ),
        name="pack_qg",
    )(q, g, w)


def pilot_pick(shift):
    where_to = lax.broadcasted_iota(jnp.int32, (PILS, HD), 0) * SLOT + shift.astype(F32).astype(jnp.int32)
    lane = lax.broadcasted_iota(jnp.int32, (PILS, HD), 1)
    picks = [jnp.where(lane + part * HD == where_to, 1.0, 0.0) for part in range(ROWS // HD)]
    return jnp.concatenate(picks, axis=1).astype(BF)


def window_scores(i, q, k_all, k_pil, labk_ref, labq_ref):
    label_q = labq_ref[i]
    key_at = lax.broadcasted_iota(jnp.int32, (ROWS, ROWS), 0)
    query_at = lax.broadcasted_iota(jnp.int32, (ROWS, ROWS), 1)
    scores = []
    for part in range(3):
        admit = labk_ref[i + part][:, :1] == label_q
        if part == 0:
            admit = admit & (key_at >= query_at)
        elif part == 2:
            admit = admit & (key_at <= query_at)
        scores.append(jnp.where(admit, mm(k_all[i + part], q, 1, 1), -jnp.inf))
    return scores + [mm(k_pil[...], q, 1, 1)]


def block_of(b, kv_ref, left_ref, right_ref):
    if b == 0:
        return left_ref[:ROWS], left_ref[ROWS:]
    if b == BLOCKS - 1:
        return right_ref[:ROWS], right_ref[ROWS:]
    return kv_ref[b - 1, :ROWS], kv_ref[b - 1, ROWS : 2 * ROWS]


def forward_kernel(
    kv_ref, q_ref, left_ref, right_ref, labk_ref, labq_ref,
    att_ref, stat_ref, k_pil, v_pil,
    k_all, vt_all, vt_pil,
):
    i = pl.program_id(0)

    @pl.when(i == 0)
    def _():
        for b in range(BLOCKS):
            kb, vb = block_of(b, kv_ref, left_ref, right_ref)
            k_all[b] = kb
            vt_all[b] = vb.T
            if 0 < b < BLOCKS - 1:
                pick = pilot_pick(kv_ref[b - 1, 2 * ROWS :])
                at = slice((b - 1) * PILS, b * PILS)
                k_pil[at] = mm(pick, kb, 1, 0).astype(BF)
                v_pil[at] = mm(pick, vb, 1, 0).astype(BF)
        vt_pil[...] = v_pil[...].T

    scores = window_scores(i, q_ref[i], k_all, k_pil, labk_ref, labq_ref)
    factor = SCALE * LOG2E
    top = functools.reduce(jnp.maximum, [jnp.max(s, axis=0, keepdims=True) for s in scores])
    top = top * factor
    exps = [jnp.exp2(s * factor - top) for s in scores]
    inverse = 1.0 / functools.reduce(jnp.add, [jnp.sum(e, axis=0, keepdims=True) for e in exps])
    stat_ref[i] = jnp.concatenate([top, inverse], axis=0)
    vts = [vt_all[i + part] for part in range(3)] + [vt_pil[...]]
    att_t = functools.reduce(
        jnp.add, [mm(vt, (e * inverse).astype(BF), 1, 0) for vt, e in zip(vts, exps)]
    )
    att_ref[i] = att_t.T.astype(BF)


def backward_kernel(
    kv_ref, q_ref, left_ref, right_ref, labk_ref, labq_ref, ga_ref, att_ref, stat_ref, k_pil, v_pil,
    dq_ref, dkv_ref, dleft_ref, dright_ref,
    k_all, v_all, kt_all, kt_pil, dk_all, dv_all, dk_pil, dv_pil,
):
    i = pl.program_id(0)

    @pl.when(i == 0)
    def _():
        for b in range(BLOCKS):
            kb, vb = block_of(b, kv_ref, left_ref, right_ref)
            k_all[b] = kb
            v_all[b] = vb
            kt_all[b] = kb.T
        kt_pil[...] = k_pil[...].T
        dk_all[...] = jnp.zeros_like(dk_all)
        dv_all[...] = jnp.zeros_like(dv_all)
        dk_pil[...] = jnp.zeros_like(dk_pil)
        dv_pil[...] = jnp.zeros_like(dv_pil)

    q = q_ref[i]
    ga = ga_ref[i]
    scores = window_scores(i, q, k_all, k_pil, labk_ref, labq_ref)
    top, inverse = stat_ref[i][:1], stat_ref[i][1:]
    product = ga.astype(F32) * att_ref[i].astype(F32)
    delta = jnp.sum(product.T, axis=0, keepdims=True)
    vals = [v_all[i + part] for part in range(3)] + [v_pil[...]]
    kts = [kt_all[i + part] for part in range(3)] + [kt_pil[...]]
    dq_t = jnp.zeros((HD, ROWS), F32)
    for part in range(4):
        prob = jnp.exp2(scores[part] * (SCALE * LOG2E) - top) * inverse
        dprob = mm(vals[part], ga, 1, 1)
        dscore = (prob * (dprob - delta)).astype(BF)
        dq_t = dq_t + mm(kts[part], dscore, 1, 0)
        dk = mm(dscore, q, 1, 0)
        dv = mm(prob.astype(BF), ga, 1, 0)
        if part < 3:
            dk_all[i + part] += dk
            dv_all[i + part] += dv
        else:
            dk_pil[...] += dk
            dv_pil[...] += dv
    dq_ref[i] = (dq_t * SCALE).T.astype(BF)

    @pl.when(i == SHARDS - 1)
    def _():
        for sh in range(SHARDS):
            pick = pilot_pick(kv_ref[sh, 2 * ROWS :])
            at = slice(sh * PILS, (sh + 1) * PILS)
            for which, (own, pil, by) in enumerate(((dk_all, dk_pil, SCALE), (dv_all, dv_pil, 1.0))):
                fine = pil[at]
                high = fine.astype(BF)
                low = (fine - high.astype(F32)).astype(BF)
                total = own[sh + 1] + (mm(pick, high, 0, 0) + mm(pick, low, 0, 0))
                dkv_ref[sh, which * ROWS : (which + 1) * ROWS] = (total * by).astype(BF)
        for ref, b in ((dleft_ref, 0), (dright_ref, BLOCKS - 1)):
            ref[:ROWS] = (dk_all[b] * SCALE).astype(BF)
            ref[ROWS:] = dv_all[b].astype(BF)


def whole(shape):
    return pl.BlockSpec(shape, lambda i: (0,) * len(shape))


def over_blocks(kernel, name, ins, outs, scratch, matmuls, room):
    return pl.pallas_call(
        kernel,
        grid=(SHARDS,),
        in_specs=[whole(a.shape) for a in ins],
        out_specs=[whole(o.shape) for o in outs],
        out_shape=outs,
        scratch_shapes=scratch,
        compiler_params=pltpu.CompilerParams(vmem_limit_bytes=room << 20),
        cost_estimate=pl.CostEstimate(
            flops=matmuls * 2 * FRAME_ROWS * 4 * ROWS * HD,
            bytes_accessed=8 << 20,
            transcendentals=FRAME_ROWS * 4 * ROWS,
        ),
        name=name,
    )(*ins)


def like(*shape, dtype=BF):
    return jax.ShapeDtypeStruct(shape, dtype)


def forward(ins):
    outs = [like(SHARDS, ROWS, HD), like(SHARDS, 2, ROWS, dtype=F32)]
    outs += [like(SHARDS * PILS, HD)] * 2
    scratch = [
        pltpu.VMEM((BLOCKS, ROWS, HD), BF),
        pltpu.VMEM((BLOCKS, HD, ROWS), BF),
        pltpu.VMEM((HD, SHARDS * PILS), BF),
    ]
    return over_blocks(forward_kernel, "forward", ins, outs, scratch, 2, 60)


def backward(ins):
    outs = [like(SHARDS, ROWS, HD), like(SHARDS, 2 * ROWS, HD)] + [like(2 * ROWS, HD)] * 2
    scratch = [
        pltpu.VMEM((BLOCKS, ROWS, HD), BF),
        pltpu.VMEM((BLOCKS, ROWS, HD), BF),
        pltpu.VMEM((BLOCKS, HD, ROWS), BF),
        pltpu.VMEM((HD, SHARDS * PILS), BF),
        pltpu.VMEM((BLOCKS, ROWS, HD), F32),
        pltpu.VMEM((BLOCKS, ROWS, HD), F32),
        pltpu.VMEM((SHARDS * PILS, HD), F32),
        pltpu.VMEM((SHARDS * PILS, HD), F32),
    ]
    return over_blocks(backward_kernel, "backward", ins, outs, scratch, 5, 60)


def mix_kernel(att_ref, w_ref, mixed_ref):
    att = jnp.concatenate([att_ref[h] for h in range(HEADS)], axis=1)
    mixed_ref[...] = mm(att, w_ref[...], 1, 0).astype(BF)


def mix(att, w):
    width = w.shape[1]
    return pl.pallas_call(
        mix_kernel,
        grid=(4,),
        in_specs=[whole(att.shape), pl.BlockSpec((width, width // 4), lambda n: (0, n))],
        out_specs=pl.BlockSpec((ROWS, width // 4), lambda n: (0, n)),
        out_shape=like(ROWS, width),
        cost_estimate=pl.CostEstimate(
            flops=2 * ROWS * width * width, bytes_accessed=3 << 20, transcendentals=0
        ),
        name="mix",
    )(att, w)


def share_kernel(heads_ref, att_ref, g_ref, *refs):
    total = mm(att_ref[0], g_ref[...], 0, 0)
    if len(refs) == 2:
        total = total + refs[0][0].astype(F32)
    refs[-1][0] = total.astype(refs[-1].dtype)


def share_of(att, g, heads, got, dtype):
    width, count = g.shape[1], heads.shape[0]
    block = (1, HD, width)
    in_specs = [
        pl.BlockSpec((1, ROWS, HD), lambda n, heads: (heads[n], 0, 0)),
        pl.BlockSpec((ROWS, width), lambda n, heads: (0, 0)),
    ]
    ins = [heads, att, g]
    if got is not None:
        in_specs.append(pl.BlockSpec(block, lambda n, heads: (heads[n] // 2, 0, 0)))
        ins.append(got)
    return pl.pallas_call(
        share_kernel,
        grid_spec=pltpu.PrefetchScalarGridSpec(
            num_scalar_prefetch=1,
            grid=(count,),
            in_specs=in_specs,
            out_specs=pl.BlockSpec(block, lambda n, heads: (n, 0, 0)),
        ),
        out_shape=like(count, HD, width, dtype=dtype),
        cost_estimate=pl.CostEstimate(
            flops=2 * count * ROWS * HD * width, bytes_accessed=2 << 20, transcendentals=0
        ),
        name="share",
    )(*ins)


def halved(value, dim, axis, bit):
    count = lax.axis_size(axis)
    size = value.shape[dim] // 2
    upper = (lax.axis_index(axis) >> bit) & 1 == 1
    low = lax.slice_in_dim(value, 0, size, axis=dim)
    high = lax.slice_in_dim(value, size, 2 * size, axis=dim)
    out = jnp.where(upper, low, high).astype(BF)
    got = lax.ppermute(out, axis, [(j, j ^ (1 << bit)) for j in range(count)])
    return jnp.where(upper, high, low) + got.astype(F32)


def scattered(value, dim, axes):
    count = lax.axis_size(axes)
    me = lax.axis_index(axes)

    def part(at):
        return lax.dynamic_index_in_dim(value, at, dim, keepdims=False)

    total = part(me)
    for apart in range(1, count):
        out = part(me ^ apart).astype(BF)
        total = total + lax.ppermute(out, axes, [(j, j ^ apart) for j in range(count)]).astype(F32)
    return total


def to_heads(x):
    return lax.all_to_all(x, FRAME, 0, 0, tiled=True)


def joined(x):
    return jnp.transpose(x, (1, 0, 2)).reshape(ROWS, HEADS * HD)


def on_device(askers, lookups, contents, cotangent, w, comb_shift, label):
    q, k, v, g = askers[0], lookups[0], contents[0], cotangent[0]
    frame = lax.axis_index(FRAMES)
    ups = [(j, j + 1) for j in range(lax.axis_size(FRAMES) - 1)]
    downs = [(j, i) for i, j in ups]

    kv = to_heads(pack_kv(k, v, comb_shift))
    left = lax.ppermute(kv[SHARDS - 1, : 2 * ROWS], FRAMES, ups)
    right = lax.ppermute(kv[0, : 2 * ROWS], FRAMES, downs)
    q, ga = pack_qg(q, g, w)
    q, kv = lax.optimization_barrier((q, kv))
    q = to_heads(q)
    q, ga, left, right = lax.optimization_barrier((q, ga, left, right))

    label = jnp.pad(label, (HALF_SPAN, HALF_SPAN), constant_values=-1)
    label = lax.dynamic_slice_in_dim(label, frame * FRAME_ROWS, BLOCKS * ROWS, 0)
    labk = jnp.broadcast_to(label.reshape(BLOCKS, ROWS, 1), (BLOCKS, ROWS, HD))
    labq = label[HALF_SPAN : HALF_SPAN + FRAME_ROWS].reshape(SHARDS, 1, ROWS)

    frame_ins = (kv, q, left, right, labk, labq)
    att, stats, k_pil, v_pil = forward(frame_ins)
    ga = to_heads(ga)
    att_rows = to_heads(att)
    dq, dkv, dleft, dright = backward(frame_ins + (ga, att, stats, k_pil, v_pil))
    att_rows, dq, dkv, dleft, dright = lax.optimization_barrier((att_rows, dq, dkv, dleft, dright))
    from_right = lax.ppermute(dleft, FRAMES, downs)
    from_left = lax.ppermute(dright, FRAMES, ups)

    core, z_bit = lax.axis_index("c"), lax.axis_index("zl") & 1
    head = jnp.arange(4, dtype=jnp.int32) * 2
    share = share_of(att_rows, g, head + (1 - core), None, BF)
    got = lax.ppermute(share, "c", [(0, 1), (1, 0)])
    mine = jnp.arange(2, dtype=jnp.int32) * 4 + core
    send = share_of(att_rows, g, mine + 2 * (1 - z_bit), got, BF)
    send, from_left, from_right = lax.optimization_barrier((send, from_left, from_right))
    keep = share_of(att_rows, g, mine + 2 * z_bit, got, F32)
    got = lax.ppermute(send, "zl", [(j, j ^ 1) for j in range(4)])
    share = keep + got.astype(F32)

    dq = to_heads(dq)
    first = dkv[:1].astype(F32) + from_left.astype(F32)[None]
    last = dkv[SHARDS - 1 :].astype(F32) + from_right.astype(F32)[None]
    dkv = jnp.concatenate([first.astype(BF), dkv[1 : SHARDS - 1], last.astype(BF)], axis=0)
    share, dq, dkv = lax.optimization_barrier((share, dq, dkv))
    dkv = to_heads(dkv)
    mixed = mix(att_rows, w)
    share = halved(share, 0, "zl", 1)[0]
    share, dkv, mixed = lax.optimization_barrier((share, dkv, mixed))

    width = share.shape[-1]
    share = scattered(share.reshape(2, 4, 16, width), 1, ("xh", "xl"))
    share = halved(share, 0, "zh", 0)
    share = scattered(share.reshape(4, 4, width), 0, ("y",))
    weight_grad = share * (1.0 / math.sqrt(8 * 32 * ROWS))
    return (
        mixed[None],
        joined(dq)[None],
        joined(dkv[:, :ROWS])[None],
        joined(dkv[:, ROWS:])[None],
        weight_grad,
    )


def solution(mesh):
    fine = Mesh(mesh.devices.reshape(4, 2, 2, 2, 2, 4), ("zl", "c", "zh", "xh", "xl", "y"))
    dp, seq = ("zl", "c"), ("zh", "xh", "xl", "y")
    rows = P(dp, seq, None)
    return jax.shard_map(
        on_device,
        mesh=fine,
        in_specs=(rows, rows, rows, rows, P(), P(seq, None), P()),
        out_specs=(rows, rows, rows, rows, P(dp + seq, None)),
        check_vma=False,
    )
```

```python
import functools
import math

import jax
import jax.numpy as jnp
from jax import lax
from jax.experimental import pallas as pl
from jax.experimental.pallas import tpu as pltpu
from jax.sharding import Mesh, PartitionSpec as P

HEADS = 8
HALF_SPAN = 256
SHARDS = 8
ROWS = 256
HD = 128
PILS = 32
SLOT = ROWS // PILS
FRAME_ROWS = SHARDS * ROWS
BLOCKS = SHARDS + 2
KV_ROWS = 2 * ROWS + PILS
BF = jnp.bfloat16
F32 = jnp.float32

FRAME = ("xl", "y")
FRAMES = ("zh", "xh")
SCALE = 1.0 / math.sqrt(HD)
LOG2E = math.log2(math.e)


def mm(a, b, ca, cb):
    return lax.dot_general(a, b, (((ca,), (cb,)), ((), ())), preferred_element_type=F32)


def pack_kv_kernel(k_ref, v_ref, s_ref, o_ref):
    down = lax.broadcasted_iota(jnp.int32, (PILS, PILS), 0)
    along = lax.broadcasted_iota(jnp.int32, (PILS, PILS), 1)
    shift = jnp.where(down == along, s_ref[...].astype(F32), 0.0)
    shift = jnp.broadcast_to(jnp.sum(shift, axis=1, keepdims=True), (PILS, HD)).astype(BF)
    for n in range(o_ref.shape[0]):
        columns = slice(n * HD, (n + 1) * HD)
        o_ref[n, :ROWS] = k_ref[:, columns]
        o_ref[n, ROWS : 2 * ROWS] = v_ref[:, columns]
        o_ref[n, 2 * ROWS :] = shift


def pack_kv(k, v, comb_shift):
    some = 4
    return pl.pallas_call(
        pack_kv_kernel,
        grid=(HEADS // some,),
        in_specs=[
            pl.BlockSpec((ROWS, some * HD), lambda h: (0, h)),
            pl.BlockSpec((ROWS, some * HD), lambda h: (0, h)),
            pl.BlockSpec((1, PILS), lambda h: (0, 0)),
        ],
        out_specs=pl.BlockSpec((some, KV_ROWS, HD), lambda h: (h, 0, 0)),
        out_shape=jax.ShapeDtypeStruct((HEADS, KV_ROWS, HD), BF),
        name="pack_kv",
    )(k, v, comb_shift)


def pack_qg_kernel(q_ref, g_ref, w_ref, o_ref):
    grad = mm(g_ref[...], w_ref[...], 1, 1).astype(BF)
    for n in range(o_ref.shape[0]):
        columns = slice(n * HD, (n + 1) * HD)
        o_ref[n, :ROWS] = q_ref[:, columns]
        o_ref[n, ROWS:] = grad[:, columns]


def pack_qg(q, g, w):
    width = g.shape[1]
    some = 2
    return pl.pallas_call(
        pack_qg_kernel,
        grid=(HEADS // some,),
        in_specs=[
            pl.BlockSpec((ROWS, some * HD), lambda h: (0, h)),
            pl.BlockSpec((ROWS, width), lambda h: (0, 0)),
            pl.BlockSpec((some * HD, width), lambda h: (h, 0)),
        ],
        out_specs=pl.BlockSpec((some, 2 * ROWS, HD), lambda h: (h, 0, 0)),
        out_shape=jax.ShapeDtypeStruct((HEADS, 2 * ROWS, HD), BF),
        cost_estimate=pl.CostEstimate(
            flops=2 * ROWS * width * width, bytes_accessed=5 << 20, transcendentals=0
        ),
        name="pack_qg",
    )(q, g, w)


def pilot_pick(shift):
    where_to = lax.broadcasted_iota(jnp.int32, (PILS, HD), 0) * SLOT + shift.astype(F32).astype(jnp.int32)
    lane = lax.broadcasted_iota(jnp.int32, (PILS, HD), 1)
    picks = [jnp.where(lane + part * HD == where_to, 1.0, 0.0) for part in range(ROWS // HD)]
    return jnp.concatenate(picks, axis=1).astype(BF)


def window_scores(i, q, k_all, k_pil, label_ref, label_col):
    label_q = label_ref[i + 1]
    key_at = lax.broadcasted_iota(jnp.int32, (ROWS, ROWS), 0)
    query_at = lax.broadcasted_iota(jnp.int32, (ROWS, ROWS), 1)
    scores = []
    for part in range(3):
        admit = label_col[i + part][:, :1] == label_q
        if part == 0:
            admit = admit & (key_at >= query_at)
        elif part == 2:
            admit = admit & (key_at <= query_at)
        scores.append(jnp.where(admit, mm(k_all[i + part], q, 1, 1), -jnp.inf))
    return scores + [mm(k_pil[...], q, 1, 1)]


def block_of(b, kv_ref, left_ref, right_ref):
    if b == 0:
        return left_ref[:ROWS], left_ref[ROWS:]
    if b == BLOCKS - 1:
        return right_ref[:ROWS], right_ref[ROWS:]
    return kv_ref[b - 1, :ROWS], kv_ref[b - 1, ROWS : 2 * ROWS]


def forward_kernel(
    kv_ref, q_ref, left_ref, right_ref, label_ref,
    att_ref, stat_ref, k_pil, v_pil,
    k_all, vt_all, vt_pil, label_col,
):
    i = pl.program_id(0)

    @pl.when(i == 0)
    def _():
        for b in range(BLOCKS):
            kb, vb = block_of(b, kv_ref, left_ref, right_ref)
            k_all[b] = kb
            label_col[b] = jnp.broadcast_to(label_ref[b], (HD, ROWS)).T
            vt_all[b] = vb.T
            if 0 < b < BLOCKS - 1:
                pick = pilot_pick(kv_ref[b - 1, 2 * ROWS :])
                at = slice((b - 1) * PILS, b * PILS)
                k_pil[at] = mm(pick, kb, 1, 0).astype(BF)
                v_pil[at] = mm(pick, vb, 1, 0).astype(BF)
        vt_pil[...] = v_pil[...].T

    scores = window_scores(i, q_ref[i], k_all, k_pil, label_ref, label_col)
    factor = SCALE * LOG2E
    top = functools.reduce(jnp.maximum, [jnp.max(s, axis=0, keepdims=True) for s in scores])
    top = top * factor
    exps = [jnp.exp2(s * factor - top) for s in scores]
    inverse = 1.0 / functools.reduce(jnp.add, [jnp.sum(e, axis=0, keepdims=True) for e in exps])
    stat_ref[i] = jnp.concatenate([top, inverse], axis=0)
    vts = [vt_all[i + part] for part in range(3)] + [vt_pil[...]]
    att_t = functools.reduce(
        jnp.add, [mm(vt, (e * inverse).astype(BF), 1, 0) for vt, e in zip(vts, exps)]
    )
    att_ref[i] = att_t.T.astype(BF)


def backward_kernel(
    kv_ref, q_ref, left_ref, right_ref, label_ref, ga_ref, att_ref, stat_ref, k_pil, v_pil,
    dq_ref, dkv_ref, dleft_ref, dright_ref,
    k_all, v_all, kt_all, kt_pil, dk_all, dv_all, dk_pil, dv_pil, label_col,
):
    i = pl.program_id(0)

    @pl.when(i == 0)
    def _():
        for b in range(BLOCKS):
            kb, vb = block_of(b, kv_ref, left_ref, right_ref)
            k_all[b] = kb
            label_col[b] = jnp.broadcast_to(label_ref[b], (HD, ROWS)).T
            v_all[b] = vb
            kt_all[b] = kb.T
        kt_pil[...] = k_pil[...].T
        dk_all[...] = jnp.zeros_like(dk_all)
        dv_all[...] = jnp.zeros_like(dv_all)
        dk_pil[...] = jnp.zeros_like(dk_pil)
        dv_pil[...] = jnp.zeros_like(dv_pil)

    q = q_ref[i]
    ga = ga_ref[i]
    scores = window_scores(i, q, k_all, k_pil, label_ref, label_col)
    top, inverse = stat_ref[i][:1], stat_ref[i][1:]
    product = ga.astype(F32) * att_ref[i].astype(F32)
    delta = jnp.sum(product.T, axis=0, keepdims=True)
    vals = [v_all[i + part] for part in range(3)] + [v_pil[...]]
    kts = [kt_all[i + part] for part in range(3)] + [kt_pil[...]]
    dq_t = jnp.zeros((HD, ROWS), F32)
    for part in range(4):
        prob = jnp.exp2(scores[part] * (SCALE * LOG2E) - top) * inverse
        dprob = mm(vals[part], ga, 1, 1)
        dscore = (prob * (dprob - delta)).astype(BF)
        dq_t = dq_t + mm(kts[part], dscore, 1, 0)
        dk = mm(dscore, q, 1, 0)
        dv = mm(prob.astype(BF), ga, 1, 0)
        if part < 3:
            dk_all[i + part] += dk
            dv_all[i + part] += dv
        else:
            dk_pil[...] += dk
            dv_pil[...] += dv
    dq_ref[i] = (dq_t * SCALE).T.astype(BF)

    @pl.when(i == SHARDS - 1)
    def _():
        for sh in range(SHARDS):
            pick = pilot_pick(kv_ref[sh, 2 * ROWS :])
            at = slice(sh * PILS, (sh + 1) * PILS)
            for which, (own, pil, by) in enumerate(((dk_all, dk_pil, SCALE), (dv_all, dv_pil, 1.0))):
                fine = pil[at]
                high = fine.astype(BF)
                low = (fine - high.astype(F32)).astype(BF)
                total = own[sh + 1] + (mm(pick, high, 0, 0) + mm(pick, low, 0, 0))
                dkv_ref[sh, which * ROWS : (which + 1) * ROWS] = (total * by).astype(BF)
        for ref, b in ((dleft_ref, 0), (dright_ref, BLOCKS - 1)):
            ref[:ROWS] = (dk_all[b] * SCALE).astype(BF)
            ref[ROWS:] = dv_all[b].astype(BF)


def whole(shape):
    return pl.BlockSpec(shape, lambda i: (0,) * len(shape))


def over_blocks(kernel, name, ins, outs, scratch, matmuls, room):
    in_specs = [whole(a.shape) for a in ins]
    for at, half in ((1, 0), (5, 1))[: len(ins) // 5]:
        in_specs[at] = pl.BlockSpec((SHARDS, ROWS, HD), lambda i, half=half: (0, half, 0))
    return pl.pallas_call(
        kernel,
        grid=(SHARDS,),
        in_specs=in_specs,
        out_specs=[whole(o.shape) for o in outs],
        out_shape=outs,
        scratch_shapes=scratch,
        compiler_params=pltpu.CompilerParams(vmem_limit_bytes=room << 20),
        cost_estimate=pl.CostEstimate(
            flops=matmuls * 2 * FRAME_ROWS * 4 * ROWS * HD,
            bytes_accessed=8 << 20,
            transcendentals=FRAME_ROWS * 4 * ROWS,
        ),
        name=name,
    )(*ins)


def like(*shape, dtype=BF):
    return jax.ShapeDtypeStruct(shape, dtype)


def forward(ins):
    outs = [like(SHARDS, ROWS, HD), like(SHARDS, 2, ROWS, dtype=F32)]
    outs += [like(SHARDS * PILS, HD)] * 2
    scratch = [
        pltpu.VMEM((BLOCKS, ROWS, HD), BF),
        pltpu.VMEM((BLOCKS, HD, ROWS), BF),
        pltpu.VMEM((HD, SHARDS * PILS), BF),
        pltpu.VMEM((BLOCKS, ROWS, HD), F32),
    ]
    return over_blocks(forward_kernel, "forward", ins, outs, scratch, 2, 60)


def backward(ins):
    outs = [like(SHARDS, ROWS, HD), like(SHARDS, 2 * ROWS, HD)] + [like(2 * ROWS, HD)] * 2
    scratch = [
        pltpu.VMEM((BLOCKS, ROWS, HD), BF),
        pltpu.VMEM((BLOCKS, ROWS, HD), BF),
        pltpu.VMEM((BLOCKS, HD, ROWS), BF),
        pltpu.VMEM((HD, SHARDS * PILS), BF),
        pltpu.VMEM((BLOCKS, ROWS, HD), F32),
        pltpu.VMEM((BLOCKS, ROWS, HD), F32),
        pltpu.VMEM((SHARDS * PILS, HD), F32),
        pltpu.VMEM((SHARDS * PILS, HD), F32),
        pltpu.VMEM((BLOCKS, ROWS, HD), F32),
    ]
    return over_blocks(backward_kernel, "backward", ins, outs, scratch, 5, 60)


def mix_kernel(att_ref, w_ref, mixed_ref):
    att = jnp.concatenate([att_ref[h] for h in range(HEADS)], axis=1)
    mixed_ref[...] = mm(att, w_ref[...], 1, 0).astype(BF)


def mix(att, w):
    width = w.shape[1]
    return pl.pallas_call(
        mix_kernel,
        grid=(4,),
        in_specs=[whole(att.shape), pl.BlockSpec((width, width // 4), lambda n: (0, n))],
        out_specs=pl.BlockSpec((ROWS, width // 4), lambda n: (0, n)),
        out_shape=like(ROWS, width),
        cost_estimate=pl.CostEstimate(
            flops=2 * ROWS * width * width, bytes_accessed=3 << 20, transcendentals=0
        ),
        name="mix",
    )(att, w)


def share_kernel(heads_ref, att_ref, g_ref, *refs):
    total = mm(att_ref[0], g_ref[...], 0, 0)
    if len(refs) == 2:
        total = total + refs[0][0].astype(F32)
    refs[-1][0] = total.astype(refs[-1].dtype)


def share_of(att, g, heads, got, dtype):
    width, count = g.shape[1], heads.shape[0]
    block = (1, HD, width)
    in_specs = [
        pl.BlockSpec((1, ROWS, HD), lambda n, heads: (heads[n], 0, 0)),
        pl.BlockSpec((ROWS, width), lambda n, heads: (0, 0)),
    ]
    ins = [heads, att, g]
    if got is not None:
        in_specs.append(pl.BlockSpec(block, lambda n, heads: (heads[n] // 2, 0, 0)))
        ins.append(got)
    return pl.pallas_call(
        share_kernel,
        grid_spec=pltpu.PrefetchScalarGridSpec(
            num_scalar_prefetch=1,
            grid=(count,),
            in_specs=in_specs,
            out_specs=pl.BlockSpec(block, lambda n, heads: (n, 0, 0)),
        ),
        out_shape=like(count, HD, width, dtype=dtype),
        cost_estimate=pl.CostEstimate(
            flops=2 * count * ROWS * HD * width, bytes_accessed=2 << 20, transcendentals=0
        ),
        name="share",
    )(*ins)


def halved(value, dim, axis, bit):
    count = lax.axis_size(axis)
    size = value.shape[dim] // 2
    upper = (lax.axis_index(axis) >> bit) & 1 == 1
    low = lax.slice_in_dim(value, 0, size, axis=dim)
    high = lax.slice_in_dim(value, size, 2 * size, axis=dim)
    out = jnp.where(upper, low, high).astype(BF)
    got = lax.ppermute(out, axis, [(j, j ^ (1 << bit)) for j in range(count)])
    return jnp.where(upper, high, low) + got.astype(F32)


def scattered(value, dim, axes):
    count = lax.axis_size(axes)
    me = lax.axis_index(axes)

    def part(at):
        return lax.dynamic_index_in_dim(value, at, dim, keepdims=False)

    total = part(me)
    for apart in range(1, count):
        out = part(me ^ apart).astype(BF)
        total = total + lax.ppermute(out, axes, [(j, j ^ apart) for j in range(count)]).astype(F32)
    return total


def to_heads(x):
    return lax.all_to_all(x, FRAME, 0, 0, tiled=True)


def joined(x):
    return jnp.transpose(x, (1, 0, 2)).reshape(ROWS, HEADS * HD)


def on_device(askers, lookups, contents, cotangent, w, comb_shift, label):
    q, k, v, g = askers[0], lookups[0], contents[0], cotangent[0]
    frame = lax.axis_index(FRAMES)
    ups = [(j, j + 1) for j in range(lax.axis_size(FRAMES) - 1)]
    downs = [(j, i) for i, j in ups]

    kv = to_heads(pack_kv(k, v, comb_shift))
    left = lax.ppermute(kv[SHARDS - 1, : 2 * ROWS], FRAMES, ups)
    right = lax.ppermute(kv[0, : 2 * ROWS], FRAMES, downs)
    qg = pack_qg(q, g, w)
    qg, kv = lax.optimization_barrier((qg, kv))
    qg = to_heads(qg)

    label = jnp.pad(label, (HALF_SPAN, HALF_SPAN), constant_values=-1)
    label = lax.dynamic_slice_in_dim(label, frame * FRAME_ROWS, BLOCKS * ROWS, 0)
    label = label.astype(F32).reshape(BLOCKS, 1, ROWS)

    frame_ins = (kv, qg, left, right, label)
    att, stats, k_pil, v_pil = forward(frame_ins)
    att_rows = to_heads(att)
    dq, dkv, dleft, dright = backward(frame_ins + (qg, att, stats, k_pil, v_pil))
    att_rows, dq, dkv, dleft, dright = lax.optimization_barrier((att_rows, dq, dkv, dleft, dright))
    from_right = lax.ppermute(dleft, FRAMES, downs)
    from_left = lax.ppermute(dright, FRAMES, ups)

    core, z_bit = lax.axis_index("c"), lax.axis_index("zl") & 1
    head = jnp.arange(4, dtype=jnp.int32) * 2
    share = share_of(att_rows, g, head + (1 - core), None, BF)
    got = lax.ppermute(share, "c", [(0, 1), (1, 0)])
    mine = jnp.arange(2, dtype=jnp.int32) * 4 + core
    send = share_of(att_rows, g, mine + 2 * (1 - z_bit), got, BF)
    keep = share_of(att_rows, g, mine + 2 * z_bit, got, F32)
    got = lax.ppermute(send, "zl", [(j, j ^ 1) for j in range(4)])
    share = keep + got.astype(F32)

    dq = to_heads(dq)
    first = dkv[:1].astype(F32) + from_left.astype(F32)[None]
    last = dkv[SHARDS - 1 :].astype(F32) + from_right.astype(F32)[None]
    dkv = jnp.concatenate([first.astype(BF), dkv[1 : SHARDS - 1], last.astype(BF)], axis=0)
    share, dq, dkv = lax.optimization_barrier((share, dq, dkv))
    dkv = to_heads(dkv)
    mixed = mix(att_rows, w)
    share = halved(share, 0, "zl", 1)[0]
    share, dkv, mixed = lax.optimization_barrier((share, dkv, mixed))

    width = share.shape[-1]
    share = scattered(share.reshape(2, 4, 16, width), 1, ("xh", "xl"))
    share = halved(share, 0, "zh", 0)
    share = scattered(share.reshape(4, 4, width), 0, ("y",))
    weight_grad = share * (1.0 / math.sqrt(8 * 32 * ROWS))
    return (
        mixed[None],
        joined(dq)[None],
        joined(dkv[:, :ROWS])[None],
        joined(dkv[:, ROWS:])[None],
        weight_grad,
    )


def solution(mesh):
    fine = Mesh(mesh.devices.reshape(4, 2, 2, 2, 2, 4), ("zl", "c", "zh", "xh", "xl", "y"))
    dp, seq = ("zl", "c"), ("zh", "xh", "xl", "y")
    rows = P(dp, seq, None)
    return jax.shard_map(
        on_device,
        mesh=fine,
        in_specs=(rows, rows, rows, rows, P(), P(seq, None), P()),
        out_specs=(rows, rows, rows, rows, P(dp + seq, None)),
        check_vma=False,
    )
```

```python
import functools
import math

import jax
import jax.numpy as jnp
from jax import lax
from jax.experimental import pallas as pl
from jax.experimental.pallas import tpu as pltpu
from jax.sharding import Mesh, PartitionSpec as P

HEADS = 8
HALF_SPAN = 256
SHARDS = 8
ROWS = 256
HD = 128
PILS = 32
SLOT = ROWS // PILS
FRAME_ROWS = SHARDS * ROWS
BLOCKS = SHARDS + 2
KV_ROWS = 2 * ROWS + PILS
BF = jnp.bfloat16
F32 = jnp.float32

FRAME = ("xl", "y")
FRAMES = ("zh", "xh")
SCALE = 1.0 / math.sqrt(HD)
LOG2E = math.log2(math.e)


def mm(a, b, ca, cb):
    return lax.dot_general(a, b, (((ca,), (cb,)), ((), ())), preferred_element_type=F32)


def pack_kv_kernel(k_ref, v_ref, s_ref, o_ref):
    down = lax.broadcasted_iota(jnp.int32, (PILS, PILS), 0)
    along = lax.broadcasted_iota(jnp.int32, (PILS, PILS), 1)
    shift = jnp.where(down == along, s_ref[...].astype(F32), 0.0)
    shift = jnp.broadcast_to(jnp.sum(shift, axis=1, keepdims=True), (PILS, HD)).astype(BF)
    for n in range(o_ref.shape[0]):
        columns = slice(n * HD, (n + 1) * HD)
        o_ref[n, :ROWS] = k_ref[:, columns]
        o_ref[n, ROWS : 2 * ROWS] = v_ref[:, columns]
        o_ref[n, 2 * ROWS :] = shift


def pack_kv(k, v, comb_shift):
    some = 4
    return pl.pallas_call(
        pack_kv_kernel,
        grid=(HEADS // some,),
        in_specs=[
            pl.BlockSpec((ROWS, some * HD), lambda h: (0, h)),
            pl.BlockSpec((ROWS, some * HD), lambda h: (0, h)),
            pl.BlockSpec((1, PILS), lambda h: (0, 0)),
        ],
        out_specs=pl.BlockSpec((some, KV_ROWS, HD), lambda h: (h, 0, 0)),
        out_shape=jax.ShapeDtypeStruct((HEADS, KV_ROWS, HD), BF),
        name="pack_kv",
    )(k, v, comb_shift)


def pack_qg_kernel(q_ref, g_ref, w_ref, o_ref):
    grad = mm(g_ref[...], w_ref[...], 1, 1).astype(BF)
    for n in range(o_ref.shape[0]):
        columns = slice(n * HD, (n + 1) * HD)
        o_ref[n, :ROWS] = q_ref[:, columns]
        o_ref[n, ROWS:] = grad[:, columns]


def pack_qg(q, g, w):
    width = g.shape[1]
    some = 2
    return pl.pallas_call(
        pack_qg_kernel,
        grid=(HEADS // some,),
        in_specs=[
            pl.BlockSpec((ROWS, some * HD), lambda h: (0, h)),
            pl.BlockSpec((ROWS, width), lambda h: (0, 0)),
            pl.BlockSpec((some * HD, width), lambda h: (h, 0)),
        ],
        out_specs=pl.BlockSpec((some, 2 * ROWS, HD), lambda h: (h, 0, 0)),
        out_shape=jax.ShapeDtypeStruct((HEADS, 2 * ROWS, HD), BF),
        cost_estimate=pl.CostEstimate(
            flops=2 * ROWS * width * width, bytes_accessed=5 << 20, transcendentals=0
        ),
        name="pack_qg",
    )(q, g, w)


def pilot_pick(shift):
    where_to = lax.broadcasted_iota(jnp.int32, (PILS, HD), 0) * SLOT + shift.astype(F32).astype(jnp.int32)
    lane = lax.broadcasted_iota(jnp.int32, (PILS, HD), 1)
    picks = [jnp.where(lane + part * HD == where_to, 1.0, 0.0) for part in range(ROWS // HD)]
    return jnp.concatenate(picks, axis=1).astype(BF)


def window_scores(i, q, k_all, k_pil, label_ref, label_col):
    label_q = label_ref[i + 1]
    key_at = lax.broadcasted_iota(jnp.int32, (ROWS, ROWS), 0)
    query_at = lax.broadcasted_iota(jnp.int32, (ROWS, ROWS), 1)
    scores = []
    for part in range(3):
        admit = label_col[i + part][:, :1] == label_q
        if part == 0:
            admit = admit & (key_at >= query_at)
        elif part == 2:
            admit = admit & (key_at <= query_at)
        scores.append(jnp.where(admit, mm(k_all[i + part], q, 1, 1), -jnp.inf))
    return scores + [mm(k_pil[...], q, 1, 1)]


def block_of(b, kv_ref, left_ref, right_ref):
    if b == 0:
        return left_ref[:ROWS], left_ref[ROWS:]
    if b == BLOCKS - 1:
        return right_ref[:ROWS], right_ref[ROWS:]
    return kv_ref[b - 1, :ROWS], kv_ref[b - 1, ROWS : 2 * ROWS]


def forward_kernel(
    kv_ref, q_ref, left_ref, right_ref, label_ref,
    att_ref, stat_ref, k_pil, v_pil,
    k_all, vt_all, vt_pil, label_col,
):
    i = pl.program_id(0)

    @pl.when(i == 0)
    def _():
        for b in range(BLOCKS):
            kb, vb = block_of(b, kv_ref, left_ref, right_ref)
            k_all[b] = kb
            label_col[b] = jnp.broadcast_to(label_ref[b], (HD, ROWS)).T
            vt_all[b] = vb.T
            if 0 < b < BLOCKS - 1:
                pick = pilot_pick(kv_ref[b - 1, 2 * ROWS :])
                at = slice((b - 1) * PILS, b * PILS)
                k_pil[at] = mm(pick, kb, 1, 0).astype(BF)
                v_pil[at] = mm(pick, vb, 1, 0).astype(BF)
        vt_pil[...] = v_pil[...].T

    scores = window_scores(i, q_ref[i], k_all, k_pil, label_ref, label_col)
    factor = SCALE * LOG2E
    top = functools.reduce(jnp.maximum, [jnp.max(s, axis=0, keepdims=True) for s in scores])
    top = top * factor
    exps = [jnp.exp2(s * factor - top) for s in scores]
    inverse = 1.0 / functools.reduce(jnp.add, [jnp.sum(e, axis=0, keepdims=True) for e in exps])
    stat_ref[i] = jnp.concatenate([top, inverse], axis=0)
    vts = [vt_all[i + part] for part in range(3)] + [vt_pil[...]]
    att_t = functools.reduce(
        jnp.add, [mm(vt, (e * inverse).astype(BF), 1, 0) for vt, e in zip(vts, exps)]
    )
    att_ref[i] = att_t.T.astype(BF)


def backward_kernel(
    kv_ref, q_ref, left_ref, right_ref, label_ref, ga_ref, att_ref, stat_ref, k_pil, v_pil,
    dq_ref, dkv_ref, dleft_ref, dright_ref,
    k_all, v_all, kt_all, kt_pil, dk_all, dv_all, dk_pil, dv_pil, label_col,
):
    i = pl.program_id(0)

    @pl.when(i == 0)
    def _():
        for b in range(BLOCKS):
            kb, vb = block_of(b, kv_ref, left_ref, right_ref)
            k_all[b] = kb
            label_col[b] = jnp.broadcast_to(label_ref[b], (HD, ROWS)).T
            v_all[b] = vb
            kt_all[b] = kb.T
        kt_pil[...] = k_pil[...].T
        dk_all[...] = jnp.zeros_like(dk_all)
        dv_all[...] = jnp.zeros_like(dv_all)
        dk_pil[...] = jnp.zeros_like(dk_pil)
        dv_pil[...] = jnp.zeros_like(dv_pil)

    q = q_ref[i]
    ga = ga_ref[i]
    scores = window_scores(i, q, k_all, k_pil, label_ref, label_col)
    top, inverse = stat_ref[i][:1], stat_ref[i][1:]
    product = ga.astype(F32) * att_ref[i].astype(F32)
    delta = jnp.sum(product.T, axis=0, keepdims=True)
    vals = [v_all[i + part] for part in range(3)] + [v_pil[...]]
    kts = [kt_all[i + part] for part in range(3)] + [kt_pil[...]]
    dq_t = jnp.zeros((HD, ROWS), F32)
    for part in range(4):
        prob = jnp.exp2(scores[part] * (SCALE * LOG2E) - top) * inverse
        dprob = mm(vals[part], ga, 1, 1)
        dscore = (prob * (dprob - delta)).astype(BF)
        dq_t = dq_t + mm(kts[part], dscore, 1, 0)
        dk = mm(dscore, q, 1, 0)
        dv = mm(prob.astype(BF), ga, 1, 0)
        if part < 3:
            dk_all[i + part] += dk
            dv_all[i + part] += dv
        else:
            dk_pil[...] += dk
            dv_pil[...] += dv
    dq_ref[i] = (dq_t * SCALE).T.astype(BF)

    @pl.when(i == SHARDS - 1)
    def _():
        for sh in range(SHARDS):
            pick = pilot_pick(kv_ref[sh, 2 * ROWS :])
            at = slice(sh * PILS, (sh + 1) * PILS)
            for which, (own, pil, by) in enumerate(((dk_all, dk_pil, SCALE), (dv_all, dv_pil, 1.0))):
                fine = pil[at]
                high = fine.astype(BF)
                low = (fine - high.astype(F32)).astype(BF)
                total = own[sh + 1] + (mm(pick, high, 0, 0) + mm(pick, low, 0, 0))
                dkv_ref[sh, which * ROWS : (which + 1) * ROWS] = (total * by).astype(BF)
        for ref, b in ((dleft_ref, 0), (dright_ref, BLOCKS - 1)):
            ref[:ROWS] = (dk_all[b] * SCALE).astype(BF)
            ref[ROWS:] = dv_all[b].astype(BF)


def whole(shape):
    return pl.BlockSpec(shape, lambda i: (0,) * len(shape))


def over_blocks(kernel, name, ins, outs, scratch, matmuls, room):
    in_specs = [whole(a.shape) for a in ins]
    for at, half in ((1, 0), (5, 1))[: len(ins) // 5]:
        in_specs[at] = pl.BlockSpec((SHARDS, ROWS, HD), lambda i, half=half: (0, half, 0))
    return pl.pallas_call(
        kernel,
        grid=(SHARDS,),
        in_specs=in_specs,
        out_specs=[whole(o.shape) for o in outs],
        out_shape=outs,
        scratch_shapes=scratch,
        compiler_params=pltpu.CompilerParams(vmem_limit_bytes=room << 20),
        cost_estimate=pl.CostEstimate(
            flops=matmuls * 2 * FRAME_ROWS * 4 * ROWS * HD,
            bytes_accessed=8 << 20,
            transcendentals=FRAME_ROWS * 4 * ROWS,
        ),
        name=name,
    )(*ins)


def like(*shape, dtype=BF):
    return jax.ShapeDtypeStruct(shape, dtype)


def forward(ins):
    outs = [like(SHARDS, ROWS, HD), like(SHARDS, 2, ROWS, dtype=F32)]
    outs += [like(SHARDS * PILS, HD)] * 2
    scratch = [
        pltpu.VMEM((BLOCKS, ROWS, HD), BF),
        pltpu.VMEM((BLOCKS, HD, ROWS), BF),
        pltpu.VMEM((HD, SHARDS * PILS), BF),
        pltpu.VMEM((BLOCKS, ROWS, HD), F32),
    ]
    return over_blocks(forward_kernel, "forward", ins, outs, scratch, 2, 60)


def backward(ins):
    outs = [like(SHARDS, ROWS, HD), like(SHARDS, 2 * ROWS, HD)] + [like(2 * ROWS, HD)] * 2
    scratch = [
        pltpu.VMEM((BLOCKS, ROWS, HD), BF),
        pltpu.VMEM((BLOCKS, ROWS, HD), BF),
        pltpu.VMEM((BLOCKS, HD, ROWS), BF),
        pltpu.VMEM((HD, SHARDS * PILS), BF),
        pltpu.VMEM((BLOCKS, ROWS, HD), F32),
        pltpu.VMEM((BLOCKS, ROWS, HD), F32),
        pltpu.VMEM((SHARDS * PILS, HD), F32),
        pltpu.VMEM((SHARDS * PILS, HD), F32),
        pltpu.VMEM((BLOCKS, ROWS, HD), F32),
    ]
    return over_blocks(backward_kernel, "backward", ins, outs, scratch, 5, 60)


def mix_kernel(att_ref, w_ref, mixed_ref):
    att = jnp.concatenate([att_ref[h] for h in range(HEADS)], axis=1)
    mixed_ref[...] = mm(att, w_ref[...], 1, 0).astype(BF)


def mix(att, w):
    width = w.shape[1]
    return pl.pallas_call(
        mix_kernel,
        grid=(4,),
        in_specs=[whole(att.shape), pl.BlockSpec((width, width // 4), lambda n: (0, n))],
        out_specs=pl.BlockSpec((ROWS, width // 4), lambda n: (0, n)),
        out_shape=like(ROWS, width),
        cost_estimate=pl.CostEstimate(
            flops=2 * ROWS * width * width, bytes_accessed=3 << 20, transcendentals=0
        ),
        name="mix",
    )(att, w)


def share_kernel(heads_ref, att_ref, g_ref, *refs):
    total = mm(att_ref[0], g_ref[...], 0, 0)
    if len(refs) == 2:
        total = total + refs[0][0].astype(F32)
    refs[-1][0] = total.astype(refs[-1].dtype)


def share_of(att, g, heads, got, dtype):
    width, count = g.shape[1], heads.shape[0]
    block = (1, HD, width)
    in_specs = [
        pl.BlockSpec((1, ROWS, HD), lambda n, heads: (heads[n], 0, 0)),
        pl.BlockSpec((ROWS, width), lambda n, heads: (0, 0)),
    ]
    ins = [heads, att, g]
    if got is not None:
        in_specs.append(pl.BlockSpec(block, lambda n, heads: (heads[n] // 2, 0, 0)))
        ins.append(got)
    return pl.pallas_call(
        share_kernel,
        grid_spec=pltpu.PrefetchScalarGridSpec(
            num_scalar_prefetch=1,
            grid=(count,),
            in_specs=in_specs,
            out_specs=pl.BlockSpec(block, lambda n, heads: (n, 0, 0)),
        ),
        out_shape=like(count, HD, width, dtype=dtype),
        cost_estimate=pl.CostEstimate(
            flops=2 * count * ROWS * HD * width, bytes_accessed=2 << 20, transcendentals=0
        ),
        name="share",
    )(*ins)


def halved(value, dim, axis, bit):
    count = lax.axis_size(axis)
    size = value.shape[dim] // 2
    upper = (lax.axis_index(axis) >> bit) & 1 == 1
    low = lax.slice_in_dim(value, 0, size, axis=dim)
    high = lax.slice_in_dim(value, size, 2 * size, axis=dim)
    out = jnp.where(upper, low, high).astype(BF)
    got = lax.ppermute(out, axis, [(j, j ^ (1 << bit)) for j in range(count)])
    return jnp.where(upper, high, low) + got.astype(F32)


def scattered(value, dim, axes):
    count = lax.axis_size(axes)
    me = lax.axis_index(axes)

    def part(at):
        return lax.dynamic_index_in_dim(value, at, dim, keepdims=False)

    total = part(me)
    for apart in range(1, count):
        out = part(me ^ apart).astype(BF)
        total = total + lax.ppermute(out, axes, [(j, j ^ apart) for j in range(count)]).astype(F32)
    return total


def to_heads(x):
    return lax.all_to_all(x, FRAME, 0, 0, tiled=True)


def joined(x):
    return jnp.transpose(x, (1, 0, 2)).reshape(ROWS, HEADS * HD)


def on_device(askers, lookups, contents, cotangent, w, comb_shift, label):
    q, k, v, g = askers[0], lookups[0], contents[0], cotangent[0]
    frame = lax.axis_index(FRAMES)
    ups = [(j, j + 1) for j in range(lax.axis_size(FRAMES) - 1)]
    downs = [(j, i) for i, j in ups]

    kv = to_heads(pack_kv(k, v, comb_shift))
    left = lax.ppermute(kv[SHARDS - 1, : 2 * ROWS], FRAMES, ups)
    right = lax.ppermute(kv[0, : 2 * ROWS], FRAMES, downs)
    qg = pack_qg(q, g, w)
    qg, kv = lax.optimization_barrier((qg, kv))
    qg = to_heads(qg)

    label = jnp.pad(label, (HALF_SPAN, HALF_SPAN), constant_values=-1)
    label = lax.dynamic_slice_in_dim(label, frame * FRAME_ROWS, BLOCKS * ROWS, 0)
    label = label.astype(F32).reshape(BLOCKS, 1, ROWS)

    frame_ins = (kv, qg, left, right, label)
    att, stats, k_pil, v_pil = forward(frame_ins)
    att_rows = to_heads(att)
    dq, dkv, dleft, dright = backward(frame_ins + (qg, att, stats, k_pil, v_pil))
    att_rows, dq, dkv, dleft, dright = lax.optimization_barrier((att_rows, dq, dkv, dleft, dright))
    from_right = lax.ppermute(dleft, FRAMES, downs)
    from_left = lax.ppermute(dright, FRAMES, ups)

    core, z_bit = lax.axis_index("c"), lax.axis_index("zl") & 1
    head = jnp.arange(4, dtype=jnp.int32) * 2
    share = share_of(att_rows, g, head + (1 - core), None, BF)
    got = lax.ppermute(share, "c", [(0, 1), (1, 0)])
    mine = jnp.arange(2, dtype=jnp.int32) * 4 + core
    send = share_of(att_rows, g, mine + 2 * (1 - z_bit), got, BF)
    keep = share_of(att_rows, g, mine + 2 * z_bit, got, F32)
    got = lax.ppermute(send, "zl", [(j, j ^ 1) for j in range(4)])
    share = keep + got.astype(F32)

    dq = to_heads(dq)
    first = dkv[:1].astype(F32) + from_left.astype(F32)[None]
    last = dkv[SHARDS - 1 :].astype(F32) + from_right.astype(F32)[None]
    dkv = jnp.concatenate([first.astype(BF), dkv[1 : SHARDS - 1], last.astype(BF)], axis=0)
    dkv = to_heads(dkv)
    mixed = mix(att_rows, w)
    share = halved(share, 0, "zl", 1)[0]
    share, dq = lax.optimization_barrier((share, dq))

    width = share.shape[-1]
    share = scattered(share.reshape(2, 4, 16, width), 1, ("xh", "xl"))
    share, dkv, mixed = lax.optimization_barrier((share, dkv, mixed))
    share = halved(share, 0, "zh", 0)
    share = scattered(share.reshape(4, 4, width), 0, ("y",))
    weight_grad = share * (1.0 / math.sqrt(8 * 32 * ROWS))
    return (
        mixed[None],
        joined(dq)[None],
        joined(dkv[:, :ROWS])[None],
        joined(dkv[:, ROWS:])[None],
        weight_grad,
    )


def solution(mesh):
    fine = Mesh(mesh.devices.reshape(4, 2, 2, 2, 2, 4), ("zl", "c", "zh", "xh", "xl", "y"))
    dp, seq = ("zl", "c"), ("zh", "xh", "xl", "y")
    rows = P(dp, seq, None)
    return jax.shard_map(
        on_device,
        mesh=fine,
        in_specs=(rows, rows, rows, rows, P(), P(seq, None), P()),
        out_specs=(rows, rows, rows, rows, P(dp + seq, None)),
        check_vma=False,
    )
```

```python
import functools
import math

import jax
import jax.numpy as jnp
from jax import lax
from jax.experimental import pallas as pl
from jax.experimental.pallas import tpu as pltpu
from jax.sharding import Mesh, PartitionSpec as P

HEADS = 8
HALF_SPAN = 256
SHARDS = 8
ROWS = 256
HD = 128
PILS = 32
SLOT = ROWS // PILS
FRAME_ROWS = SHARDS * ROWS
BLOCKS = SHARDS + 2
KV_ROWS = 2 * ROWS + PILS
BF = jnp.bfloat16
F32 = jnp.float32

FRAME = ("xl", "y")
FRAMES = ("zh", "xh")
SCALE = 1.0 / math.sqrt(HD)
LOG2E = math.log2(math.e)


def mm(a, b, ca, cb):
    return lax.dot_general(a, b, (((ca,), (cb,)), ((), ())), preferred_element_type=F32)


def pack_kv_kernel(k_ref, v_ref, s_ref, o_ref):
    down = lax.broadcasted_iota(jnp.int32, (PILS, PILS), 0)
    along = lax.broadcasted_iota(jnp.int32, (PILS, PILS), 1)
    shift = jnp.where(down == along, s_ref[...].astype(F32), 0.0)
    shift = jnp.broadcast_to(jnp.sum(shift, axis=1, keepdims=True), (PILS, HD)).astype(BF)
    for n in range(o_ref.shape[0]):
        columns = slice(n * HD, (n + 1) * HD)
        o_ref[n, :ROWS] = k_ref[:, columns]
        o_ref[n, ROWS : 2 * ROWS] = v_ref[:, columns]
        o_ref[n, 2 * ROWS :] = shift


def pack_kv(k, v, comb_shift):
    some = 4
    return pl.pallas_call(
        pack_kv_kernel,
        grid=(HEADS // some,),
        in_specs=[
            pl.BlockSpec((ROWS, some * HD), lambda h: (0, h)),
            pl.BlockSpec((ROWS, some * HD), lambda h: (0, h)),
            pl.BlockSpec((1, PILS), lambda h: (0, 0)),
        ],
        out_specs=pl.BlockSpec((some, KV_ROWS, HD), lambda h: (h, 0, 0)),
        out_shape=jax.ShapeDtypeStruct((HEADS, KV_ROWS, HD), BF),
        name="pack_kv",
    )(k, v, comb_shift)


def pack_qg_kernel(q_ref, g_ref, w_ref, o_ref):
    grad = mm(g_ref[...], w_ref[...], 1, 1).astype(BF)
    for n in range(o_ref.shape[0]):
        columns = slice(n * HD, (n + 1) * HD)
        o_ref[n, :ROWS] = q_ref[:, columns]
        o_ref[n, ROWS:] = grad[:, columns]


def pack_qg(q, g, w):
    width = g.shape[1]
    some = 2
    return pl.pallas_call(
        pack_qg_kernel,
        grid=(HEADS // some,),
        in_specs=[
            pl.BlockSpec((ROWS, some * HD), lambda h: (0, h)),
            pl.BlockSpec((ROWS, width), lambda h: (0, 0)),
            pl.BlockSpec((some * HD, width), lambda h: (h, 0)),
        ],
        out_specs=pl.BlockSpec((some, 2 * ROWS, HD), lambda h: (h, 0, 0)),
        out_shape=jax.ShapeDtypeStruct((HEADS, 2 * ROWS, HD), BF),
        cost_estimate=pl.CostEstimate(
            flops=2 * ROWS * width * width, bytes_accessed=5 << 20, transcendentals=0
        ),
        name="pack_qg",
    )(q, g, w)


def pilot_pick(shift):
    where_to = lax.broadcasted_iota(jnp.int32, (PILS, HD), 0) * SLOT + shift.astype(F32).astype(jnp.int32)
    lane = lax.broadcasted_iota(jnp.int32, (PILS, HD), 1)
    picks = [jnp.where(lane + part * HD == where_to, 1.0, 0.0) for part in range(ROWS // HD)]
    return jnp.concatenate(picks, axis=1).astype(BF)


def window_scores(i, q, k_all, k_pil, label_ref, label_col):
    label_q = label_ref[i + 1]
    key_at = lax.broadcasted_iota(jnp.int32, (ROWS, ROWS), 0)
    query_at = lax.broadcasted_iota(jnp.int32, (ROWS, ROWS), 1)
    scores = []
    for part in range(3):
        admit = label_col[i + part][:, :1] == label_q
        if part == 0:
            admit = admit & (key_at >= query_at)
        elif part == 2:
            admit = admit & (key_at <= query_at)
        scores.append(jnp.where(admit, mm(k_all[i + part], q, 1, 1), -jnp.inf))
    return scores + [mm(k_pil[...], q, 1, 1)]


def block_of(b, kv_ref, left_ref, right_ref):
    if b == 0:
        return left_ref[:ROWS], left_ref[ROWS:]
    if b == BLOCKS - 1:
        return right_ref[:ROWS], right_ref[ROWS:]
    return kv_ref[b - 1, :ROWS], kv_ref[b - 1, ROWS : 2 * ROWS]


def forward_kernel(
    kv_ref, q_ref, left_ref, right_ref, label_ref,
    att_ref, stat_ref, k_pil, v_pil,
    k_all, vt_all, vt_pil, label_col,
):
    i = pl.program_id(0)

    @pl.when(i == 0)
    def _():
        for b in range(BLOCKS):
            kb, vb = block_of(b, kv_ref, left_ref, right_ref)
            k_all[b] = kb
            label_col[b] = jnp.broadcast_to(label_ref[b], (HD, ROWS)).T
            vt_all[b] = vb.T
            if 0 < b < BLOCKS - 1:
                pick = pilot_pick(kv_ref[b - 1, 2 * ROWS :])
                at = slice((b - 1) * PILS, b * PILS)
                k_pil[at] = mm(pick, kb, 1, 0).astype(BF)
                v_pil[at] = mm(pick, vb, 1, 0).astype(BF)
        vt_pil[...] = v_pil[...].T

    scores = window_scores(i, q_ref[i], k_all, k_pil, label_ref, label_col)
    factor = SCALE * LOG2E
    top = functools.reduce(jnp.maximum, [jnp.max(s, axis=0, keepdims=True) for s in scores])
    top = top * factor
    exps = [jnp.exp2(s * factor - top) for s in scores]
    inverse = 1.0 / functools.reduce(jnp.add, [jnp.sum(e, axis=0, keepdims=True) for e in exps])
    stat_ref[i] = jnp.concatenate([top, inverse], axis=0)
    vts = [vt_all[i + part] for part in range(3)] + [vt_pil[...]]
    att_t = functools.reduce(
        jnp.add, [mm(vt, (e * inverse).astype(BF), 1, 0) for vt, e in zip(vts, exps)]
    )
    att_ref[i] = att_t.T.astype(BF)


def backward_kernel(
    kv_ref, q_ref, left_ref, right_ref, label_ref, ga_ref, att_ref, stat_ref, k_pil, v_pil,
    dq_ref, dkv_ref, dleft_ref, dright_ref,
    k_all, v_all, kt_all, kt_pil, dk_all, dv_all, dk_pil, dv_pil, label_col,
):
    i = pl.program_id(0)

    @pl.when(i == 0)
    def _():
        for b in range(BLOCKS):
            kb, vb = block_of(b, kv_ref, left_ref, right_ref)
            k_all[b] = kb
            label_col[b] = jnp.broadcast_to(label_ref[b], (HD, ROWS)).T
            v_all[b] = vb
            kt_all[b] = kb.T
        kt_pil[...] = k_pil[...].T
        dk_all[...] = jnp.zeros_like(dk_all)
        dv_all[...] = jnp.zeros_like(dv_all)
        dk_pil[...] = jnp.zeros_like(dk_pil)
        dv_pil[...] = jnp.zeros_like(dv_pil)

    q = q_ref[i]
    ga = ga_ref[i]
    scores = window_scores(i, q, k_all, k_pil, label_ref, label_col)
    top, inverse = stat_ref[i][:1], stat_ref[i][1:]
    product = ga.astype(F32) * att_ref[i].astype(F32)
    delta = jnp.sum(product.T, axis=0, keepdims=True)
    vals = [v_all[i + part] for part in range(3)] + [v_pil[...]]
    kts = [kt_all[i + part] for part in range(3)] + [kt_pil[...]]
    dq_t = jnp.zeros((HD, ROWS), F32)
    for part in range(4):
        prob = jnp.exp2(scores[part] * (SCALE * LOG2E) - top) * inverse
        dprob = mm(vals[part], ga, 1, 1)
        dscore = (prob * (dprob - delta)).astype(BF)
        dq_t = dq_t + mm(kts[part], dscore, 1, 0)
        dk = mm(dscore, q, 1, 0)
        dv = mm(prob.astype(BF), ga, 1, 0)
        if part < 3:
            dk_all[i + part] += dk
            dv_all[i + part] += dv
        else:
            dk_pil[...] += dk
            dv_pil[...] += dv
    dq_ref[i] = (dq_t * SCALE).T.astype(BF)

    @pl.when(i == SHARDS - 1)
    def _():
        for sh in range(SHARDS):
            pick = pilot_pick(kv_ref[sh, 2 * ROWS :])
            at = slice(sh * PILS, (sh + 1) * PILS)
            for which, (own, pil, by) in enumerate(((dk_all, dk_pil, SCALE), (dv_all, dv_pil, 1.0))):
                fine = pil[at]
                high = fine.astype(BF)
                low = (fine - high.astype(F32)).astype(BF)
                total = own[sh + 1] + (mm(pick, high, 0, 0) + mm(pick, low, 0, 0))
                dkv_ref[sh, which * ROWS : (which + 1) * ROWS] = (total * by).astype(BF)
        for ref, b in ((dleft_ref, 0), (dright_ref, BLOCKS - 1)):
            ref[:ROWS] = (dk_all[b] * SCALE).astype(BF)
            ref[ROWS:] = dv_all[b].astype(BF)


def whole(shape):
    return pl.BlockSpec(shape, lambda i: (0,) * len(shape))


def over_blocks(kernel, name, ins, outs, scratch, matmuls, room):
    in_specs = [whole(a.shape) for a in ins]
    for at, half in ((1, 0), (5, 1))[: len(ins) // 5]:
        in_specs[at] = pl.BlockSpec((SHARDS, ROWS, HD), lambda i, half=half: (0, half, 0))
    return pl.pallas_call(
        kernel,
        grid=(SHARDS,),
        in_specs=in_specs,
        out_specs=[whole(o.shape) for o in outs],
        out_shape=outs,
        scratch_shapes=scratch,
        compiler_params=pltpu.CompilerParams(vmem_limit_bytes=room << 20),
        cost_estimate=pl.CostEstimate(
            flops=matmuls * 2 * FRAME_ROWS * 4 * ROWS * HD,
            bytes_accessed=8 << 20,
            transcendentals=FRAME_ROWS * 4 * ROWS,
        ),
        name=name,
    )(*ins)


def like(*shape, dtype=BF):
    return jax.ShapeDtypeStruct(shape, dtype)


def forward(ins):
    outs = [like(SHARDS, ROWS, HD), like(SHARDS, 2, ROWS, dtype=F32)]
    outs += [like(SHARDS * PILS, HD)] * 2
    scratch = [
        pltpu.VMEM((BLOCKS, ROWS, HD), BF),
        pltpu.VMEM((BLOCKS, HD, ROWS), BF),
        pltpu.VMEM((HD, SHARDS * PILS), BF),
        pltpu.VMEM((BLOCKS, ROWS, HD), F32),
    ]
    return over_blocks(forward_kernel, "forward", ins, outs, scratch, 2, 60)


def backward(ins):
    outs = [like(SHARDS, ROWS, HD), like(SHARDS, 2 * ROWS, HD)] + [like(2 * ROWS, HD)] * 2
    scratch = [
        pltpu.VMEM((BLOCKS, ROWS, HD), BF),
        pltpu.VMEM((BLOCKS, ROWS, HD), BF),
        pltpu.VMEM((BLOCKS, HD, ROWS), BF),
        pltpu.VMEM((HD, SHARDS * PILS), BF),
        pltpu.VMEM((BLOCKS, ROWS, HD), F32),
        pltpu.VMEM((BLOCKS, ROWS, HD), F32),
        pltpu.VMEM((SHARDS * PILS, HD), F32),
        pltpu.VMEM((SHARDS * PILS, HD), F32),
        pltpu.VMEM((BLOCKS, ROWS, HD), F32),
    ]
    return over_blocks(backward_kernel, "backward", ins, outs, scratch, 5, 60)


def mix_kernel(att_ref, w_ref, mixed_ref):
    att = jnp.concatenate([att_ref[h] for h in range(HEADS)], axis=1)
    mixed_ref[...] = mm(att, w_ref[...], 1, 0).astype(BF)


def mix(att, w):
    width = w.shape[1]
    return pl.pallas_call(
        mix_kernel,
        grid=(4,),
        in_specs=[whole(att.shape), pl.BlockSpec((width, width // 4), lambda n: (0, n))],
        out_specs=pl.BlockSpec((ROWS, width // 4), lambda n: (0, n)),
        out_shape=like(ROWS, width),
        cost_estimate=pl.CostEstimate(
            flops=2 * ROWS * width * width, bytes_accessed=3 << 20, transcendentals=0
        ),
        name="mix",
    )(att, w)


def share_kernel(heads_ref, att_ref, g_ref, *refs):
    total = mm(att_ref[0], g_ref[...], 0, 0)
    if len(refs) == 2:
        total = total + refs[0][0].astype(F32)
    refs[-1][0] = total.astype(refs[-1].dtype)


def share_of(att, g, heads, got, dtype):
    width, count = g.shape[1], heads.shape[0]
    block = (1, HD, width)
    in_specs = [
        pl.BlockSpec((1, ROWS, HD), lambda n, heads: (heads[n], 0, 0)),
        pl.BlockSpec((ROWS, width), lambda n, heads: (0, 0)),
    ]
    ins = [heads, att, g]
    if got is not None:
        in_specs.append(pl.BlockSpec(block, lambda n, heads: (heads[n] // 2, 0, 0)))
        ins.append(got)
    return pl.pallas_call(
        share_kernel,
        grid_spec=pltpu.PrefetchScalarGridSpec(
            num_scalar_prefetch=1,
            grid=(count,),
            in_specs=in_specs,
            out_specs=pl.BlockSpec(block, lambda n, heads: (n, 0, 0)),
        ),
        out_shape=like(count, HD, width, dtype=dtype),
        cost_estimate=pl.CostEstimate(
            flops=2 * count * ROWS * HD * width, bytes_accessed=2 << 20, transcendentals=0
        ),
        name="share",
    )(*ins)


def halved(value, dim, axis, bit):
    count = lax.axis_size(axis)
    size = value.shape[dim] // 2
    upper = (lax.axis_index(axis) >> bit) & 1 == 1
    low = lax.slice_in_dim(value, 0, size, axis=dim)
    high = lax.slice_in_dim(value, size, 2 * size, axis=dim)
    out = jnp.where(upper, low, high).astype(BF)
    got = lax.ppermute(out, axis, [(j, j ^ (1 << bit)) for j in range(count)])
    return jnp.where(upper, high, low) + got.astype(F32)


def scattered(value, dim, axes):
    count = lax.axis_size(axes)
    me = lax.axis_index(axes)

    def part(at):
        return lax.dynamic_index_in_dim(value, at, dim, keepdims=False)

    total = part(me)
    for apart in range(1, count):
        out = part(me ^ apart).astype(BF)
        total = total + lax.ppermute(out, axes, [(j, j ^ apart) for j in range(count)]).astype(F32)
    return total


def to_heads(x):
    return lax.all_to_all(x, FRAME, 0, 0, tiled=True)


def joined(x):
    return jnp.transpose(x, (1, 0, 2)).reshape(ROWS, HEADS * HD)


def on_device(askers, lookups, contents, cotangent, w, comb_shift, label):
    q, k, v, g = askers[0], lookups[0], contents[0], cotangent[0]
    frame = lax.axis_index(FRAMES)
    ups = [(j, j + 1) for j in range(lax.axis_size(FRAMES) - 1)]
    downs = [(j, i) for i, j in ups]

    kv = to_heads(pack_kv(k, v, comb_shift))
    left = lax.ppermute(kv[SHARDS - 1, : 2 * ROWS], FRAMES, ups)
    right = lax.ppermute(kv[0, : 2 * ROWS], FRAMES, downs)
    qg = pack_qg(q, g, w)
    qg, kv = lax.optimization_barrier((qg, kv))
    qg = to_heads(qg)

    label = jnp.pad(label, (HALF_SPAN, HALF_SPAN), constant_values=-1)
    label = lax.dynamic_slice_in_dim(label, frame * FRAME_ROWS, BLOCKS * ROWS, 0)
    label = label.astype(F32).reshape(BLOCKS, 1, ROWS)

    frame_ins = (kv, qg, left, right, label)
    att, stats, k_pil, v_pil = forward(frame_ins)
    att_rows = to_heads(att)
    dq, dkv, dleft, dright = backward(frame_ins + (qg, att, stats, k_pil, v_pil))
    att_rows, dq, dkv, dleft, dright = lax.optimization_barrier((att_rows, dq, dkv, dleft, dright))

    core, z_bit = lax.axis_index("c"), lax.axis_index("zl") & 1
    head = jnp.arange(4, dtype=jnp.int32) * 2
    share = share_of(att_rows, g, head + (1 - core), None, BF)
    got = lax.ppermute(share, "c", [(0, 1), (1, 0)])
    mine = jnp.arange(2, dtype=jnp.int32) * 4 + core
    send = share_of(att_rows, g, mine + 2 * (1 - z_bit), got, BF)
    keep = share_of(att_rows, g, mine + 2 * z_bit, got, F32)
    got = lax.ppermute(send, "zl", [(j, j ^ 1) for j in range(4)])
    share = keep + got.astype(F32)

    upper = (lax.axis_index("zl") >> 1) & 1 == 1
    out = jnp.where(upper, share[0], share[1]).astype(BF)
    from_right = lax.ppermute(dleft, FRAMES, downs)
    from_left = lax.ppermute(dright, FRAMES, ups)
    out, from_left, from_right, dq = lax.optimization_barrier((out, from_left, from_right, dq))
    got = lax.ppermute(out, "zl", [(j, j ^ 2) for j in range(4)])
    dq = to_heads(dq)
    first = dkv[:1].astype(F32) + from_left.astype(F32)[None]
    last = dkv[SHARDS - 1 :].astype(F32) + from_right.astype(F32)[None]
    dkv = jnp.concatenate([first.astype(BF), dkv[1 : SHARDS - 1], last.astype(BF)], axis=0)
    dkv = to_heads(dkv)
    mixed = mix(att_rows, w)
    share = jnp.where(upper, share[1], share[0]) + got.astype(F32)

    width = share.shape[-1]
    share = scattered(share.reshape(2, 4, 16, width), 1, ("xh", "xl"))
    share, dq, mixed = lax.optimization_barrier((share, dq, mixed))
    share = halved(share, 0, "zh", 0)
    share, dkv = lax.optimization_barrier((share, dkv))
    share = scattered(share.reshape(4, 4, width), 0, ("y",))
    weight_grad = share * (1.0 / math.sqrt(8 * 32 * ROWS))
    return (
        mixed[None],
        joined(dq)[None],
        joined(dkv[:, :ROWS])[None],
        joined(dkv[:, ROWS:])[None],
        weight_grad,
    )


def solution(mesh):
    fine = Mesh(mesh.devices.reshape(4, 2, 2, 2, 2, 4), ("zl", "c", "zh", "xh", "xl", "y"))
    dp, seq = ("zl", "c"), ("zh", "xh", "xl", "y")
    rows = P(dp, seq, None)
    return jax.shard_map(
        on_device,
        mesh=fine,
        in_specs=(rows, rows, rows, rows, P(), P(seq, None), P()),
        out_specs=(rows, rows, rows, rows, P(dp + seq, None)),
        check_vma=False,
    )
```
